256 devices in a mesh: freq: 128 (over z, y_lo, x, core), col: 2 (over y_hi).
Axes of the slice: x: 4, y: 4 (y_hi: 2, y_lo: 2; y = y_hi * 2 + y_lo), z: 8, core: 2. Of those that a mesh axis runs over, the one named last changes fastest.
Arguments:
- traces: bfloat16 [1024, 1024, 1024], P('freq', 'col'), may hold values from -6 to 6
- source_row: int32 [1024], replicated, may hold values from 0 to 1023, each once
Outputs:
- multiples: bfloat16 [2, 128, 1024, 1024], P(None, 'freq', None, 'col')
The draws below stay inside these ranges and needn't reach their ends.
Inputs may be any that keep to these rules, and one draw needn't show every extreme that they name: `source_row`: a permutation of the 1024 acquisition rows.
All inputs are finite; a program needn't handle non-finite values.
Results may differ from the reference program's by a relative error of at most 0.0079.
Values may be sent and summed in bfloat16 or wider, within the bound.
No kernel may reach another device: no remote copies, remote signals or barrier semaphores. Data moves between devices by JAX's collectives and lax.ppermute only.
A program may use at most 64 MiB of HBM per device.

```python
import math
import jax
import jax.numpy as jnp
from jax import lax

NS = 1024
NR = 1024
NF = 128
NT = 1024


def shard_levels(stream_key, extent, shards, low, top_value):
    def one(axis_at, blocks):
        draws = jax.random.uniform(jax.random.fold_in(jax.random.fold_in(stream_key, 6), axis_at), (blocks,), jnp.float32, low / len(shards), top_value / len(shards))
        return jnp.repeat(jnp.exp(draws), extent[axis_at] // blocks).reshape((-1,) + (1,) * (len(extent) - axis_at - 1))

    level = one(*shards[0])
    for cut in shards[1:]:
        level = level * one(*cut)
    return level


def gaussian(key, extent, deviation, reach, split=(), dtype=jnp.bfloat16):
    factor_of = shard_levels(key, extent, split, -0.22, 0.18) if split else 1.0
    values = jax.random.normal(key, extent, jnp.float32) * deviation * factor_of
    return jnp.minimum(jnp.maximum(values, -reach), reach).astype(dtype)


def setup_inputs(seed: int = 0) -> dict:
    seeds = jax.random.split(jax.random.key(seed), 3)
    traces = gaussian(seeds[0], (NS, NR, NT), 1.0, 6.0, ((0, 128), (1, 2)))
    source_row = jax.random.permutation(seeds[1], NS).astype(jnp.int32)
    return dict(traces=traces, source_row=source_row)


def dft_table(samples, kept):
    row_index = jnp.arange(2 * kept)
    frequency = (row_index % kept)[:, None]
    sample_index = jnp.arange(samples)[None, :]
    phase = frequency * sample_index % samples
    angle = 2.0 * math.pi / samples * phase.astype(jnp.float32)
    table = jnp.where(row_index[:, None] < kept, jnp.cos(angle), -jnp.sin(angle))
    return (table / jnp.sqrt(jnp.float32(samples))).astype(jnp.bfloat16)

def real_product(first, second):
    return jnp.matmul(first.astype(jnp.float32), second.astype(jnp.float32), precision=lax.Precision.HIGHEST)

def complex_product(left, right):
    real_part = real_product(left[0], right[0]) - real_product(left[1], right[1])
    imag_part = real_product(left[0], right[1]) + real_product(left[1], right[0])
    return jnp.stack([real_part, imag_part])

def reference(traces, source_row):
    table = dft_table(NT, NF)
    spectrum = jnp.einsum('kt,srt->ksr', table.astype(jnp.float32), traces.astype(jnp.float32), precision=lax.Precision.HIGHEST)
    spectrum = spectrum.astype(jnp.bfloat16).reshape(2, NF, NS, NR)
    scale = 1.0 / math.sqrt(NS)

    def one_frequency(slab):
        arranged = slab[:, source_row, :]
        spectral = ((arranged.astype(jnp.float32) + jnp.swapaxes(arranged, 1, 2).astype(jnp.float32)) * 0.5).astype(jnp.bfloat16)
        square = (scale * complex_product(spectral, spectral)).astype(jnp.bfloat16)
        cube = scale * complex_product(spectral, square)
        return (spectral.astype(jnp.float32) - square.astype(jnp.float32) + cube).astype(jnp.bfloat16)
    multiples = lax.map(one_frequency, jnp.moveaxis(spectrum, 1, 0))
    return jnp.moveaxis(multiples, 0, 1)
```

```python
import functools
import math

import jax
import jax.numpy as jnp
from jax import lax
from jax.experimental import pallas as pl
from jax.experimental.pallas import tpu as pltpu
from jax.sharding import PartitionSpec as P

BF16 = jnp.bfloat16
F32 = jnp.float32
VMEM = pl.BlockSpec(memory_space=pltpu.VMEM)
SMEM = pl.BlockSpec(memory_space=pltpu.SMEM)


def partner(value):
    return lax.ppermute(value, "col", [(0, 1), (1, 0)])


def dft_table(samples, kept):
    row_index = jnp.arange(2 * kept)
    frequency = (row_index % kept)[:, None]
    sample_index = jnp.arange(samples)[None, :]
    phase = frequency * sample_index % samples
    angle = 2.0 * math.pi / samples * phase.astype(F32)
    table = jnp.where(row_index[:, None] < kept, jnp.cos(angle), -jnp.sin(angle))
    return (table / jnp.sqrt(jnp.float32(samples))).astype(BF16)


def dot(a, b, dims=((1,), (0,))):
    return lax.dot_general(a, b, (dims, ((), ())), preferred_element_type=F32)


NT = ((1,), (1,))


def dft_kernel(table_ref, traces_ref, out_ref, stage_ref):
    sources = traces_ref.shape[0]
    rows = table_ref.shape[0]
    for s in range(sources):
        stage_ref[pl.ds(s, rows, stride=sources), :] = dot(table_ref[...], traces_ref[s], NT)
    out_ref[...] = stage_ref[...].reshape(rows, sources, traces_ref.shape[1]).astype(BF16)


def dft(table, traces):
    rows, samples = table.shape
    sources, receivers, _ = traces.shape
    width = 128
    return pl.pallas_call(
        dft_kernel,
        grid=(receivers // width,),
        in_specs=[
            pl.BlockSpec((rows, samples), lambda j: (0, 0)),
            pl.BlockSpec((sources, width, samples), lambda j: (0, j, 0)),
        ],
        out_specs=pl.BlockSpec((rows, sources, width), lambda j: (0, 0, j)),
        out_shape=jax.ShapeDtypeStruct((rows, sources, receivers), BF16),
        scratch_shapes=[pltpu.VMEM((rows * sources, width), F32)],
        cost_estimate=pl.CostEstimate(
            flops=2 * rows * samples * sources * receivers,
            bytes_accessed=2 * (sources * receivers * samples + rows * samples + rows * sources * receivers),
            transcendentals=0,
        ),
    )(table, traces)


def arrange_kernel(pick_ref, piece_ref, own_ref, off_ref):
    owners, sources, width = piece_ref.shape
    size = owners * sources
    half = size // 2
    rows = piece_ref[...].astype(F32).reshape(size, width).astype(BF16)
    off_ref[...] = dot(pick_ref[half:, :], rows).astype(BF16)
    block = dot(pick_ref[:half, :], rows)
    eye = (
        lax.broadcasted_iota(jnp.int32, (half, half), 0) == lax.broadcasted_iota(jnp.int32, (half, half), 1)
    ).astype(BF16)
    own_ref[...] = ((block + dot(eye, block.astype(BF16), NT)) * 0.5).astype(BF16)


def arrange(pick, piece):
    owners, sources, width = piece.shape
    half = owners * sources // 2
    shape = jax.ShapeDtypeStruct((half, width), BF16)
    return pl.pallas_call(
        arrange_kernel,
        in_specs=[VMEM, VMEM],
        out_specs=[VMEM, VMEM],
        out_shape=[shape, shape],
        cost_estimate=pl.CostEstimate(flops=4 * half * 2 * half * width, bytes_accessed=12 * half * width, transcendentals=0),
    )(pick, piece)


def predict_kernel(
    scale, col_ref, own_r, own_i, off_r, off_i, their_off_r, their_off_i, their_own_r, their_own_i, out_ref, left_ref, right_ref, square_ref
):
    half = own_r.shape[0]
    size = 2 * half
    eye = (
        lax.broadcasted_iota(jnp.int32, (half, half), 0) == lax.broadcasted_iota(jnp.int32, (half, half), 1)
    ).astype(BF16)
    parts = ((own_r, off_r, their_off_r, their_own_r), (own_i, off_i, their_off_i, their_own_i))
    for part, (own, off, their_off, their_own) in enumerate(parts):
        lower = ((off[...].astype(F32) + dot(eye, their_off[...], NT)) * 0.5).astype(BF16)
        upper = ((their_off[...].astype(F32) + dot(eye, off[...], NT)) * 0.5).astype(BF16)
        at = part * size
        left_ref[:half, at : at + half] = own[...]
        left_ref[half:, at : at + half] = lower
        left_ref[:half, at + half : at + size] = upper
        left_ref[half:, at + half : at + size] = their_own[...]
        cols = slice(part * half, (part + 1) * half)
        right_ref[:half, cols] = own[...]
        right_ref[half:size, cols] = lower
        if part == 0:
            right_ref[size : size + half, half:] = own[...]
            right_ref[size + half :, half:] = lower
        else:
            right_ref[size : size + half, :half] = -own[...]
            right_ref[size + half :, :half] = -lower
    for at in range(0, size, half):
        product = (scale * dot(left_ref[at : at + half, :], right_ref[...])).astype(BF16)
        square_ref[at : at + half, :] = product
        square_ref[size + at : size + at + half, half:] = product[:, :half]
        square_ref[size + at : size + at + half, :half] = -product[:, half:]
    for number, at in enumerate((0, half)):
        product = scale * dot(left_ref[at : at + half, :], square_ref[...])
        whole = right_ref[at : at + half, :].astype(F32) - square_ref[at : at + half, :].astype(F32) + product
        whole = whole.astype(BF16)
        row = pl.multiple_of((col_ref[0] ^ number) * half, half)
        out_ref[0, 0, pl.ds(row, half), :] = whole[:, :half]
        out_ref[1, 0, pl.ds(row, half), :] = whole[:, half:]


def predict(column_half, *blocks):
    half, width = blocks[0].shape
    size = 2 * half
    return pl.pallas_call(
        functools.partial(predict_kernel, 1.0 / math.sqrt(size)),
        in_specs=[SMEM] + [VMEM] * len(blocks),
        out_specs=VMEM,
        out_shape=jax.ShapeDtypeStruct((2, 1, size, width), BF16),
        scratch_shapes=[
            pltpu.VMEM((size, 2 * size), BF16),
            pltpu.VMEM((2 * size, 2 * width), BF16),
            pltpu.VMEM((2 * size, 2 * width), BF16),
        ],
        cost_estimate=pl.CostEstimate(flops=16 * size * size * width, bytes_accessed=12 * size * width, transcendentals=0),
    )(jnp.full((1,), column_half, jnp.int32), *blocks)


def shards(traces, source_row):
    sources, receivers, samples = traces.shape
    kept = samples // 8
    size = source_row.shape[0]
    table = dft_table(samples, kept)
    column_half = lax.axis_index("col")
    order = jnp.roll(source_row, -column_half * (size // 2))
    pick = (order[:, None] == jnp.arange(size)[None, :]).astype(BF16)
    own, off = [], []
    for part in range(2):
        piece = dft(table[part * kept : (part + 1) * kept], traces)
        piece = lax.all_to_all(piece, "freq", split_axis=0, concat_axis=0, tiled=True)
        block, rest = arrange(pick, piece)
        own.append(block)
        off.append(rest)
    their_off = [partner(value) for value in off]
    their_own = [partner(value) for value in own]
    return predict(column_half, *own, *off, *their_off, *their_own)


def solution(mesh):
    in_specs = (P("freq", "col", None), P())
    out_specs = P(None, "freq", None, "col")
    return jax.shard_map(shards, mesh=mesh, in_specs=in_specs, out_specs=out_specs, check_vma=False)
```

```python
import functools
import math

import jax
import jax.numpy as jnp
import numpy as np
from jax import lax
from jax.experimental import pallas as pl
from jax.experimental.pallas import tpu as pltpu
from jax.sharding import PartitionSpec as P

BF16 = jnp.bfloat16
F32 = jnp.float32
VMEM = pl.BlockSpec(memory_space=pltpu.VMEM)
SMEM = pl.BlockSpec(memory_space=pltpu.SMEM)
NT = ((1,), (1,))
PAD = 16


def partner(value):
    return lax.ppermute(value, "col", [(0, 1), (1, 0)])


def dft_table(samples, kept):
    phase = np.arange(kept)[:, None] * np.arange(samples)[None, :] % samples
    angle = np.float32(2.0 * math.pi / samples) * phase.astype(np.float32)
    table = np.stack([np.cos(angle), -np.sin(angle)], 1).reshape(2 * kept, samples)
    return jnp.asarray(table / np.sqrt(np.float32(samples)), dtype=BF16)


def dot(a, b, dims=((1,), (0,))):
    return lax.dot_general(a, b, (dims, ((), ())), preferred_element_type=F32)


def grid_of(size):
    return lax.broadcasted_iota(jnp.int32, (size, size), 0), lax.broadcasted_iota(jnp.int32, (size, size), 1)


def turn(block):
    row, col = grid_of(block.shape[0])
    return dot((row == col).astype(BF16), block, NT)


def call(kernel, out_shape, flops, moved, vmem_mib, **rest):
    return pl.pallas_call(
        kernel,
        out_shape=out_shape,
        cost_estimate=pl.CostEstimate(flops=flops, bytes_accessed=moved, transcendentals=0),
        compiler_params=pltpu.CompilerParams(vmem_limit_bytes=vmem_mib << 20),
        **rest,
    )


def dft_kernel(table_ref, traces_ref, out_ref, stage_ref):
    sources = traces_ref.shape[0]
    blocks, _, lanes = stage_ref.shape
    rows = table_ref.shape[0]
    for s in range(sources):
        value = dot(table_ref[...], traces_ref[s], NT)
        for b in range(blocks):
            stage_ref.at[b][pl.ds(s, rows, stride=sources), :] = value[:, b * lanes : (b + 1) * lanes]
    for b in range(blocks):
        out_ref[:, :, b * lanes : (b + 1) * lanes] = stage_ref[b].reshape(rows, sources, lanes).astype(BF16)


def dft(table, traces):
    rows, samples = table.shape
    sources, receivers, _ = traces.shape
    width, lanes = 256, 128
    return call(
        dft_kernel,
        jax.ShapeDtypeStruct((rows, sources, receivers), BF16),
        2 * rows * samples * sources * receivers,
        2 * (sources * receivers * samples + rows * samples + rows * sources * receivers),
        60,
        grid=(receivers // width,),
        in_specs=[
            pl.BlockSpec((rows, samples), lambda j: (0, 0)),
            pl.BlockSpec((sources, width, samples), lambda j: (0, j, 0)),
        ],
        out_specs=pl.BlockSpec((rows, sources, width), lambda j: (0, 0, j)),
        scratch_shapes=[pltpu.VMEM((width // lanes, rows * sources, lanes), F32)],
    )(table, traces)


def rows_of(piece_ref, part):
    owners, _, sources, width = piece_ref.shape
    return piece_ref[:, part].astype(F32).reshape(owners * sources, width).astype(BF16)


def off_kernel(pick_ref, piece_ref, off_r, off_i):
    half = off_r.shape[0]
    for part, off in enumerate((off_r, off_i)):
        off[...] = dot(pick_ref[half:, :], rows_of(piece_ref, part)).astype(BF16)


def own_kernel(pick_ref, piece_ref, own_r, own_i, packed_ref):
    half = own_r.shape[0]
    for part, own in enumerate((own_r, own_i)):
        block = dot(pick_ref[:half, :], rows_of(piece_ref, part))
        own[...] = ((block + turn(block.astype(BF16))) * 0.5).astype(BF16)
    row, col = grid_of(half)
    real, imag = own_r[...].astype(F32), own_i[...].astype(F32)
    packed_ref[:half, :] = jnp.where(row >= col, real, imag).astype(BF16)
    diagonal = jnp.sum(jnp.where(row == col, imag, 0.0), axis=0, keepdims=True)
    packed_ref[half:, :] = jnp.broadcast_to(diagonal, (PAD, half)).astype(BF16)


def put_right(right_ref, real, imag):
    half = real.shape[0]
    right_ref[:half, :half] = real
    right_ref[:half, half:] = imag
    right_ref[half:, :half] = -imag
    right_ref[half:, half:] = real


def first_kernel(
    scale, own_r, own_i, off_r, off_i, their_r, their_i,
    right_low, upper_ref, square_own, part_other, cube_own, cube_other, left_own, left_low, right_own, right_square,
):
    half = own_r.shape[0]
    for part, (own, off, their) in enumerate(((own_r, off_r, their_r), (own_i, off_i, their_i))):
        cols = slice(part * half, (part + 1) * half)
        left_own[:, cols] = own[...]
        left_low[:, cols] = ((off[...].astype(F32) + turn(their[...])) * 0.5).astype(BF16)
        upper_ref[:, cols] = ((their[...].astype(F32) + turn(off[...])) * 0.5).astype(BF16)
    put_right(right_own, own_r[...], own_i[...])
    put_right(right_low, left_low[:, :half], left_low[:, half:])
    product = dot(left_own[...], right_own[...]) + dot(upper_ref[...], right_low[...])
    square_own[...] = (scale * product).astype(BF16)
    put_right(right_square, square_own[:, :half], square_own[:, half:])
    part_other[...] = dot(left_low[...], right_own[...])
    cube_own[...] = dot(left_own[...], right_square[...])
    cube_other[...] = dot(left_low[...], right_square[...])


def first(*blocks):
    half = blocks[0].shape[0]
    wide = jax.ShapeDtypeStruct((half, 2 * half), BF16)
    long = jax.ShapeDtypeStruct((half, 2 * half), F32)
    square = jax.ShapeDtypeStruct((2 * half, 2 * half), BF16)
    return call(
        functools.partial(first_kernel, 1.0 / math.sqrt(2 * half)),
        [square, wide, wide, long, long, long],
        40 * half**3,
        60 * half**2,
        32,
        in_specs=[VMEM] * 6,
        out_specs=[VMEM] * 6,
        scratch_shapes=[pltpu.VMEM((half, 2 * half), BF16)] * 2 + [pltpu.VMEM((2 * half, 2 * half), BF16)] * 2,
    )(*blocks)


def second_kernel(
    scale, col_ref, packed_ref, own_r, own_i, right_low, upper_ref, square_own, part_other, cube_own, cube_other,
    out_ref, left_other, right_square,
):
    half = own_r.shape[0]
    row, col = grid_of(half)
    packed = packed_ref[:half, :]
    turned, packed = turn(packed), packed.astype(F32)
    diagonal = packed_ref[half : half + 1, :].astype(F32)
    left_other[:, :half] = jnp.where(row >= col, packed, turned).astype(BF16)
    left_other[:, half:] = jnp.where(row < col, packed, jnp.where(row > col, turned, diagonal)).astype(BF16)
    square = (scale * (part_other[...] + dot(left_other[...], right_low[...]))).astype(BF16)
    put_right(right_square, square[:, :half], square[:, half:])
    mine = pl.multiple_of(col_ref[0] * half, half)
    other = pl.multiple_of((1 - col_ref[0]) * half, half)
    cube = scale * (cube_own[...] + dot(upper_ref[...], right_square[...]))
    for part, own in enumerate((own_r, own_i)):
        cols = slice(part * half, (part + 1) * half)
        whole = own[...].astype(F32) - square_own[:, cols].astype(F32) + cube[:, cols]
        out_ref[part, 0, pl.ds(mine, half), :] = whole.astype(BF16)
    cube = scale * (cube_other[...] + dot(left_other[...], right_square[...]))
    for part in range(2):
        cols = slice(part * half, (part + 1) * half)
        whole = right_low[:half, cols].astype(F32) - square[:, cols].astype(F32) + cube[:, cols]
        out_ref[part, 0, pl.ds(other, half), :] = whole.astype(BF16)


def second(column_half, *blocks):
    half = blocks[1].shape[0]
    return call(
        functools.partial(second_kernel, 1.0 / math.sqrt(2 * half)),
        jax.ShapeDtypeStruct((2, 1, 2 * half, half), BF16),
        24 * half**3,
        60 * half**2,
        32,
        in_specs=[SMEM] + [VMEM] * len(blocks),
        out_specs=VMEM,
        scratch_shapes=[pltpu.VMEM((half, 2 * half), BF16), pltpu.VMEM((2 * half, 2 * half), BF16)],
    )(jnp.full((1,), column_half, jnp.int32), *blocks)


def shards(traces, source_row):
    sources, receivers, samples = traces.shape
    kept = samples // 8
    size = source_row.shape[0]
    half = size // 2
    column_half = lax.axis_index("col")
    order = jnp.roll(source_row, -column_half * half)
    pick = (order[:, None] == jnp.arange(size)[None, :]).astype(BF16)
    piece = dft(dft_table(samples, kept), traces).reshape(kept, 2, sources, receivers)
    piece = lax.all_to_all(piece, "freq", split_axis=0, concat_axis=0, tiled=True)
    block = jax.ShapeDtypeStruct((half, half), BF16)
    flops = 4 * half * size * half
    off = call(off_kernel, [block] * 2, flops, 14 * half**2, 24, in_specs=[VMEM] * 2, out_specs=[VMEM] * 2)(pick, piece)
    packed = jax.ShapeDtypeStruct((half + PAD, half), BF16)
    *own, packed = call(own_kernel, [block, block, packed], flops, 14 * half**2, 24, in_specs=[VMEM] * 2, out_specs=[VMEM] * 3)(pick, piece)
    their_off = [partner(value) for value in off]
    their_packed = partner(packed)
    return second(column_half, their_packed, *own, *first(*own, *off, *their_off))


def solution(mesh):
    in_specs = (P("freq", "col", None), P())
    out_specs = P(None, "freq", None, "col")
    return jax.shard_map(shards, mesh=mesh, in_specs=in_specs, out_specs=out_specs, check_vma=False)
```

```python
import functools
import math

import jax
import jax.numpy as jnp
import numpy as np
from jax import lax
from jax.experimental import pallas as pl
from jax.experimental.pallas import tpu as pltpu
from jax.sharding import PartitionSpec as P


BF16 = jnp.bfloat16
F32 = jnp.float32
VMEM = pl.BlockSpec(memory_space=pltpu.VMEM)
SMEM = pl.BlockSpec(memory_space=pltpu.SMEM)
NT = ((1,), (1,))
PAD = 16


def partner(value):
    return lax.ppermute(value, "col", [(0, 1), (1, 0)])


WIDE, NARROW = 384, 128
NEAR, NEAR_BITS = 4, 9


def dft_table(samples, kept):
    phase = np.arange(kept)[:, None] * np.arange(samples)[None, :] % samples
    angle = np.float32(2.0 * math.pi / samples) * phase.astype(np.float32)
    table = np.stack([np.cos(angle), -np.sin(angle)], 1).reshape(2 * kept, samples)
    return jnp.asarray(table / np.sqrt(np.float32(samples)), dtype=BF16)


def dot(a, b, dims=((1,), (0,))):
    return lax.dot_general(a, b, (dims, ((), ())), preferred_element_type=F32)


def grid_of(size):
    return lax.broadcasted_iota(jnp.int32, (size, size), 0), lax.broadcasted_iota(jnp.int32, (size, size), 1)


def turn(block):
    row, col = grid_of(block.shape[1])
    return dot((row == col).astype(BF16), block, NT)


def call(kernel, out_shape, flops, moved, vmem_mib, **rest):
    return pl.pallas_call(
        kernel,
        out_shape=out_shape,
        cost_estimate=pl.CostEstimate(flops=flops, bytes_accessed=moved, transcendentals=0),
        compiler_params=pltpu.CompilerParams(vmem_limit_bytes=vmem_mib << 20),
        **rest,
    )


def far_owner(index):
    return index // 4 * 16 + index % 4 * 2


def near_bits(k):
    return k // 2 * 8 + k % 2


def dft_kernel(near_ref, table_ref, traces_ref, wide_ref, *rest):
    *narrow_refs, stage_ref = rest
    sources = traces_ref.shape[0]
    blocks, rows, lanes = stage_ref.shape
    rows //= sources
    for s in range(sources):
        value = dot(table_ref[...], traces_ref[s], NT)
        for b in range(blocks):
            stage_ref.at[b][pl.ds(s, rows, stride=sources), :] = value[:, b * lanes : (b + 1) * lanes]
    for b in range(blocks):
        wide_ref[:, :, b * lanes : (b + 1) * lanes] = stage_ref[b].reshape(rows, sources, lanes).astype(BF16)

    @pl.when(pl.program_id(0) == pl.num_programs(0) - 1)
    def _():
        step = 2 * sources
        for k, narrow_ref in enumerate(narrow_refs):
            near = near_ref[0] ^ near_bits(k)
            for index in range(narrow_ref.shape[0]):
                at = pl.multiple_of((far_owner(index) + near) * step, step)
                narrow_ref[index] = stage_ref[blocks - 1, pl.ds(at, step), :].reshape(2, sources, lanes).astype(BF16)


def dft(near, table, traces):
    rows, samples = table.shape
    sources, receivers, _ = traces.shape
    width = 2 * NARROW
    assert receivers == WIDE + NARROW == 2 * width
    wide = jax.ShapeDtypeStruct((rows, sources, WIDE), BF16)
    narrow = (rows // 2 // NEAR, 2, sources, NARROW)
    return call(
        dft_kernel,
        [wide] + [jax.ShapeDtypeStruct(narrow, BF16)] * NEAR,
        2 * rows * samples * sources * receivers,
        2 * (sources * receivers * samples + rows * samples + rows * sources * receivers),
        60,
        grid=(receivers // width,),
        in_specs=[
            SMEM,
            pl.BlockSpec((rows, samples), lambda j: (0, 0)),
            pl.BlockSpec((sources, width, samples), lambda j: (0, j, 0)),
        ],
        out_specs=[pl.BlockSpec((rows, sources, width), lambda j: (0, 0, j))]
        + [pl.BlockSpec(narrow, lambda j: (0, 0, 0, 0))] * NEAR,
        scratch_shapes=[pltpu.VMEM((2, rows * sources, NARROW), F32)],
    )(near, table, traces)


def join_kernel(*refs):
    *in_refs, out_ref = refs
    for k, in_ref in enumerate(in_refs):
        out_ref[:, k] = in_ref[...]


def join(pieces):
    count, *rest = pieces[0].shape
    shape = (count, len(pieces), *rest)
    return call(
        join_kernel,
        jax.ShapeDtypeStruct(shape, BF16),
        0,
        4 * math.prod(shape),
        60,
        in_specs=[VMEM] * len(pieces),
        out_specs=VMEM,
    )(*pieces)


def pick_rows(order_ref, at, count):
    lanes, size = 128, order_ref.shape[1]
    row = order_ref[:, at : at + count].astype(F32)
    column = jnp.broadcast_to(row, (lanes, count)).T
    lane = lax.broadcasted_iota(jnp.int32, (count, lanes), 1).astype(F32)
    picks = [jnp.where(column == lane + float(b), 1.0, 0.0).astype(BF16) for b in range(0, size, lanes)]
    return jnp.concatenate(picks, axis=1)


def rows_of(piece_ref, part):
    owners, _, sources, width = piece_ref.shape
    return piece_ref[:, part].astype(F32).reshape(owners * sources, width).astype(BF16)


def off_kernel(order_ref, piece_ref, off_ref):
    half = off_ref.shape[1]
    pick = pick_rows(order_ref, half, half)
    for part in range(2):
        off_ref[part] = dot(pick, rows_of(piece_ref, part)).astype(BF16)


def off_block(order, piece):
    half, width = order.shape[1] // 2, piece.shape[3]
    return call(
        off_kernel,
        jax.ShapeDtypeStruct((2, half, width), BF16),
        8 * half * half * width,
        14 * half * width,
        16,
        in_specs=[VMEM] * 2,
        out_specs=VMEM,
    )(order, piece)


def mix(real, imag):
    row, col = grid_of(real.shape[0])
    diagonal = jnp.sum(jnp.where(row == col, imag, 0.0), axis=0, keepdims=True)
    return jnp.where(row >= col, real, imag).astype(BF16), jnp.broadcast_to(diagonal, (PAD, real.shape[0])).astype(BF16)


def unmix(mixed, diagonal):
    row, col = grid_of(mixed.shape[0])
    turned, mixed, diagonal = turn(mixed), mixed.astype(F32), diagonal.astype(F32)
    real = jnp.where(row >= col, mixed, turned)
    imag = jnp.where(row < col, mixed, jnp.where(row > col, turned, diagonal))
    return real.astype(BF16), imag.astype(BF16)


def wide_kernel(order_ref, piece_ref, square_ref, below_ref, packed_ref):
    pick = pick_rows(order_ref, 0, WIDE + NARROW)
    parts = []
    for part in range(2):
        block = dot(pick, rows_of(piece_ref, part))
        below_ref[part] = block[WIDE:].astype(BF16)
        parts.append((block[:WIDE] + turn(block[:WIDE].astype(BF16))) * 0.5)
        square_ref[part] = parts[part].astype(BF16)
    packed_ref[:WIDE, :], packed_ref[WIDE:, :] = mix(*parts)


def wide_block(order, piece):
    half = WIDE + NARROW
    return call(
        wide_kernel,
        [jax.ShapeDtypeStruct(shape, BF16) for shape in ((2, WIDE, WIDE), (2, NARROW, WIDE), (WIDE + PAD, WIDE))],
        8 * half * half * WIDE,
        14 * half * WIDE,
        20,
        in_specs=[VMEM] * 2,
        out_specs=[VMEM] * 3,
    )(order, piece)


CUT = 48


def narrow_kernel(order_ref, piece_ref, square_ref, below_ref, own_ref, packed_ref):
    pick = pick_rows(order_ref, 0, WIDE + NARROW)
    corners = []
    for part in range(2):
        block = dot(pick, rows_of(piece_ref, part))
        beside, corner = block[:WIDE].astype(BF16), block[WIDE:]
        low = ((below_ref[part].astype(F32) + turn(beside)) * 0.5).astype(BF16)
        corners.append((corner + turn(corner.astype(BF16))) * 0.5)
        own_ref[part, :WIDE, :WIDE] = square_ref[part]
        own_ref[part, WIDE:, :WIDE] = low
        own_ref[part, :WIDE, WIDE:] = turn(low).astype(BF16)
        own_ref[part, WIDE:, WIDE:] = corners[part].astype(BF16)
        packed_ref[part * NARROW : (part + 1) * NARROW, :] = low
    mixed, diagonal = mix(*corners)
    at = 2 * NARROW
    packed_ref[at:, :NARROW] = mixed[:CUT]
    packed_ref[at:, NARROW : 2 * NARROW] = mixed[CUT : 2 * CUT]
    packed_ref[at:, 2 * NARROW :] = jnp.concatenate([mixed[2 * CUT :], diagonal], axis=0)


def narrow_block(order, piece, square, below):
    half = WIDE + NARROW
    return call(
        narrow_kernel,
        [jax.ShapeDtypeStruct(shape, BF16) for shape in ((2, half, half), (2 * NARROW + CUT, WIDE))],
        8 * half * half * NARROW,
        14 * half * half,
        20,
        in_specs=[VMEM] * 4,
        out_specs=[VMEM] * 2,
    )(order, piece, square, below)


def unpack(left_wide, left_narrow, wide_ref, narrow_ref):
    squares = unmix(wide_ref[:WIDE, :], wide_ref[WIDE : WIDE + 1, :])
    cuts = narrow_ref[2 * NARROW :, :]
    rest = NARROW - 2 * CUT
    mixed = jnp.concatenate([cuts[:, :NARROW], cuts[:, NARROW : 2 * NARROW], cuts[:rest, 2 * NARROW :]], axis=0)
    corners = unmix(mixed, cuts[rest : rest + 1, 2 * NARROW :])
    for part in range(2):
        low = narrow_ref[part * NARROW : (part + 1) * NARROW, :]
        at = slice(part * WIDE, (part + 1) * WIDE)
        left_wide[:WIDE, at] = squares[part]
        left_wide[WIDE:, at] = low
        at = slice(part * NARROW, (part + 1) * NARROW)
        left_narrow[:WIDE, at] = turn(low).astype(BF16)
        left_narrow[WIDE:, at] = corners[part]


def put_right(right_ref, real, imag):
    rows, cols = real.shape
    right_ref[:rows, :cols] = real
    right_ref[:rows, cols:] = imag
    right_ref[rows:, :cols] = -imag
    right_ref[rows:, cols:] = real


def average(block, turned):
    return ((block.astype(F32) + turn(turned)) * 0.5).astype(BF16)


def early_kernel(own_ref, off_wide, off_narrow, their_wide, right_own, upper_wide, right_wide, part_own, part_other):
    half = own_ref.shape[1]
    put_right(right_own, own_ref[0], own_ref[1])
    lows = []
    for part in range(2):
        off = jnp.concatenate([off_wide[part, :WIDE, :], off_narrow[part, :WIDE, :]], axis=1)
        lows.append(average(off, their_wide[part]))
        upper_wide[:, part * WIDE : (part + 1) * WIDE] = average(their_wide[part], off)
    put_right(right_wide, *lows)
    part_own[...] = dot(right_own[:half, :], right_own[...]) + dot(upper_wide[...], right_wide[...])
    part_other[...] = dot(right_wide[:WIDE, :], right_own[...])


def early(*blocks):
    half = WIDE + NARROW
    shapes = [
        jax.ShapeDtypeStruct((2 * half, 2 * half), BF16),
        jax.ShapeDtypeStruct((half, 2 * WIDE), BF16),
        jax.ShapeDtypeStruct((2 * WIDE, 2 * half), BF16),
        jax.ShapeDtypeStruct((half, 2 * half), F32),
        jax.ShapeDtypeStruct((WIDE, 2 * half), F32),
    ]
    return call(
        early_kernel, shapes, 24 * half**3, 60 * half**2, 24, in_specs=[VMEM] * len(blocks), out_specs=[VMEM] * len(shapes)
    )(*blocks)


def first_kernel(
    scale, off_wide, off_narrow, their_narrow, right_own, right_wide, part_own,
    upper_narrow, right_narrow, square_own, part_other, cube_own, cube_wide, cube_narrow, right_square,
):
    half = off_wide.shape[1]
    lows = []
    for part in range(2):
        off = jnp.concatenate([off_wide[part, WIDE:, :], off_narrow[part, WIDE:, :]], axis=1)
        lows.append(average(off, their_narrow[part]))
        upper_narrow[:, part * NARROW : (part + 1) * NARROW] = average(their_narrow[part], off)
    put_right(right_narrow, *lows)
    square = (scale * (part_own[...] + dot(upper_narrow[...], right_narrow[...]))).astype(BF16)
    square_own[...] = square
    put_right(right_square, square[:, :half], square[:, half:])
    part_other[...] = dot(right_narrow[:NARROW, :], right_own[...])
    cube_own[...] = dot(right_own[:half, :], right_square[...])
    cube_wide[...] = dot(right_wide[:WIDE, :], right_square[...])
    cube_narrow[...] = dot(right_narrow[:NARROW, :], right_square[...])


def first(*blocks):
    half = WIDE + NARROW
    shapes = [
        jax.ShapeDtypeStruct((half, 2 * NARROW), BF16),
        jax.ShapeDtypeStruct((2 * NARROW, 2 * half), BF16),
        jax.ShapeDtypeStruct((half, 2 * half), BF16),
        jax.ShapeDtypeStruct((NARROW, 2 * half), F32),
        jax.ShapeDtypeStruct((half, 2 * half), F32),
        jax.ShapeDtypeStruct((WIDE, 2 * half), F32),
        jax.ShapeDtypeStruct((NARROW, 2 * half), F32),
    ]
    return call(
        functools.partial(first_kernel, 1.0 / math.sqrt(2 * half)),
        shapes,
        22 * half**3,
        60 * half**2,
        28,
        in_specs=[VMEM] * len(blocks),
        out_specs=[VMEM] * len(shapes),
        scratch_shapes=[pltpu.VMEM((2 * half, 2 * half), BF16)],
    )(*blocks)


def second_kernel(
    scale, col_ref, packed_wide, packed_narrow, right_own, square_own, cube_own,
    upper_wide, right_wide, other_wide, cube_wide, upper_narrow, right_narrow, other_narrow, cube_narrow,
    out_ref, left_wide, left_narrow, next_wide, next_narrow, whole_ref, sems,
):
    half = WIDE + NARROW
    unpack(left_wide, left_narrow, packed_wide, packed_narrow)

    def product(wide, narrow):
        return dot(left_wide[...], wide[...]) + dot(left_narrow[...], narrow[...])

    def send(number, values):
        row = pl.multiple_of(lax.rem(col_ref[0] + number, 2) * half, half)
        copies = []
        for part in range(2):
            whole_ref[number, part] = values[:, part * half : (part + 1) * half].astype(BF16)
            copies.append(
                pltpu.make_async_copy(
                    whole_ref.at[number, part], out_ref.at[part, 0, pl.ds(row, half)], sems.at[2 * number + part]
                )
            )
            copies[-1].start()
        return copies

    other = jnp.concatenate([other_wide[...], other_narrow[...]], axis=0)
    square = (scale * (other + product(right_wide, right_narrow))).astype(BF16)
    put_right(next_wide, square[:WIDE, :half], square[:WIDE, half:])
    put_right(next_narrow, square[WIDE:, :half], square[WIDE:, half:])
    cube = scale * (cube_own[...] + dot(upper_wide[...], next_wide[...]) + dot(upper_narrow[...], next_narrow[...]))
    copies = send(0, right_own[:half, :].astype(F32) - square_own[...].astype(F32) + cube)
    other = jnp.concatenate([cube_wide[...], cube_narrow[...]], axis=0)
    cube = scale * (other + product(next_wide, next_narrow))
    low = jnp.concatenate([right_wide[:WIDE, :], right_narrow[:NARROW, :]], axis=0)
    copies += send(1, low.astype(F32) - square.astype(F32) + cube)
    for copy in copies:
        copy.wait()


def second(column_half, *blocks):
    half = WIDE + NARROW
    return call(
        functools.partial(second_kernel, 1.0 / math.sqrt(2 * half)),
        jax.ShapeDtypeStruct((2, 1, 2 * half, half), BF16),
        24 * half**3,
        60 * half**2,
        32,
        in_specs=[SMEM] + [VMEM] * len(blocks),
        out_specs=pl.BlockSpec(memory_space=pl.ANY),
        scratch_shapes=[
            pltpu.VMEM((half, 2 * WIDE), BF16),
            pltpu.VMEM((half, 2 * NARROW), BF16),
            pltpu.VMEM((2 * WIDE, 2 * half), BF16),
            pltpu.VMEM((2 * NARROW, 2 * half), BF16),
            pltpu.VMEM((2, 2, half, half), BF16),
            pltpu.SemaphoreType.DMA((4,)),
        ],
    )(scalar(column_half), *blocks)


def scalar(value):
    return jnp.full((1,), value, jnp.int32)


def swap(piece, groups=None):
    return lax.all_to_all(piece, "freq", split_axis=0, concat_axis=0, tiled=True, axis_index_groups=groups)


def swap_near(value, bits):
    return lax.ppermute(value, "freq", [(i, i ^ bits) for i in range(lax.axis_size("freq"))])


def body(traces, source_row):
    sources, _, samples = traces.shape
    kept = samples // 8
    size = source_row.shape[0]
    assert lax.axis_size("freq") == kept == 128
    column_half = lax.axis_index("col")
    owner = lax.axis_index("freq")
    order = jnp.roll(source_row, -column_half * (size // 2))[None, :]
    source_owner = order // sources
    apart = source_owner ^ owner
    near = (apart // 8 & 1) * 2 + (apart & 1)
    far = source_owner // 16 * 4 + (source_owner // 2 & 3)
    mixed_order = (far * NEAR + near) * sources + order % sources
    wide, *narrow = dft(scalar(owner & NEAR_BITS), dft_table(samples, kept), traces)
    wide = swap(wide.reshape(kept, 2, sources, WIDE))
    for k in range(1, NEAR):
        narrow[k] = swap_near(narrow[k], near_bits(k))
    narrow = join(narrow)
    off_wide = off_block(order, wide)
    their_off_wide = partner(off_wide)
    groups = [[far_owner(i) + near_bits(k) for i in range(kept // NEAR)] for k in range(NEAR)]
    narrow = swap(narrow, groups).reshape(kept, 2, sources, NARROW)
    square, below, packed_wide = wide_block(order, wide)
    packed_wide = partner(packed_wide)
    off_narrow = off_block(mixed_order, narrow)
    their_off_narrow = partner(off_narrow)
    own, packed_narrow = narrow_block(mixed_order, narrow, square, below)
    packed_narrow = partner(packed_narrow)
    right_own, upper_wide, right_wide, part_own, other_wide = early(own, off_wide, off_narrow, their_off_wide)
    upper_narrow, right_narrow, square_own, other_narrow, cube_own, cube_wide, cube_narrow = first(
        off_wide, off_narrow, their_off_narrow, right_own, right_wide, part_own
    )
    return second(
        column_half, packed_wide, packed_narrow, right_own, square_own, cube_own,
        upper_wide, right_wide, other_wide, cube_wide, upper_narrow, right_narrow, other_narrow, cube_narrow,
    )


def solution(mesh):
    in_specs = (P("freq", "col", None), P())
    out_specs = P(None, "freq", None, "col")
    return jax.shard_map(body, mesh=mesh, in_specs=in_specs, out_specs=out_specs, check_vma=False)
```

```python
import functools
import math

import jax
import jax.numpy as jnp
import numpy as np
from jax import lax
from jax.experimental import pallas as pl
from jax.experimental.pallas import tpu as pltpu
from jax.sharding import PartitionSpec as P


BF16 = jnp.bfloat16
F32 = jnp.float32
VMEM = pl.BlockSpec(memory_space=pltpu.VMEM)
SMEM = pl.BlockSpec(memory_space=pltpu.SMEM)
NT = ((1,), (1,))
PAD = 16


def partner(value):
    return lax.ppermute(value, "col", [(0, 1), (1, 0)])


WIDE, NARROW = 384, 128
NEAR, NEAR_BITS = 4, 9


def dft_table(samples, kept):
    phase = np.arange(kept)[:, None] * np.arange(samples)[None, :] % samples
    angle = np.float32(2.0 * math.pi / samples) * phase.astype(np.float32)
    table = np.stack([np.cos(angle), -np.sin(angle)], 1).reshape(2 * kept, samples)
    return jnp.asarray(table / np.sqrt(np.float32(samples)), dtype=BF16)


def dot(a, b, dims=((1,), (0,))):
    return lax.dot_general(a, b, (dims, ((), ())), preferred_element_type=F32)


def grid_of(size):
    return lax.broadcasted_iota(jnp.int32, (size, size), 0), lax.broadcasted_iota(jnp.int32, (size, size), 1)


def turn(block):
    return block.T.astype(F32)


def call(kernel, out_shape, flops, moved, vmem_mib, **rest):
    return pl.pallas_call(
        kernel,
        out_shape=out_shape,
        cost_estimate=pl.CostEstimate(flops=flops, bytes_accessed=moved, transcendentals=0),
        compiler_params=pltpu.CompilerParams(vmem_limit_bytes=vmem_mib << 20),
        **rest,
    )


def far_owner(index):
    return index // 4 * 16 + index % 4 * 2


def near_bits(k):
    return k // 2 * 8 + k % 2


def dft_kernel(near_ref, table_ref, traces_ref, wide_ref, *rest):
    *narrow_refs, stage_ref = rest
    sources = traces_ref.shape[0]
    blocks, rows, lanes = stage_ref.shape
    rows //= sources
    for s in range(sources):
        value = dot(table_ref[...], traces_ref[s], NT)
        for b in range(blocks):
            stage_ref.at[b][pl.ds(s, rows, stride=sources), :] = value[:, b * lanes : (b + 1) * lanes]
    for b in range(blocks):
        wide_ref[:, :, b * lanes : (b + 1) * lanes] = stage_ref[b].reshape(rows, sources, lanes).astype(BF16)

    @pl.when(pl.program_id(0) == pl.num_programs(0) - 1)
    def _():
        step = 2 * sources
        for k, narrow_ref in enumerate(narrow_refs):
            near = near_ref[0] ^ near_bits(k)
            for index in range(narrow_ref.shape[0]):
                at = pl.multiple_of((far_owner(index) + near) * step, step)
                narrow_ref[index] = stage_ref[blocks - 1, pl.ds(at, step), :].reshape(2, sources, lanes).astype(BF16)


def dft(near, table, traces):
    rows, samples = table.shape
    sources, receivers, _ = traces.shape
    width = 2 * NARROW
    assert receivers == WIDE + NARROW == 2 * width
    wide = jax.ShapeDtypeStruct((rows, sources, WIDE), BF16)
    narrow = (rows // 2 // NEAR, 2, sources, NARROW)
    return call(
        dft_kernel,
        [wide] + [jax.ShapeDtypeStruct(narrow, BF16)] * NEAR,
        2 * rows * samples * sources * receivers,
        2 * (sources * receivers * samples + rows * samples + rows * sources * receivers),
        60,
        grid=(receivers // width,),
        in_specs=[
            SMEM,
            pl.BlockSpec((rows, samples), lambda j: (0, 0)),
            pl.BlockSpec((sources, width, samples), lambda j: (0, j, 0)),
        ],
        out_specs=[pl.BlockSpec((rows, sources, width), lambda j: (0, 0, j))]
        + [pl.BlockSpec(narrow, lambda j: (0, 0, 0, 0))] * NEAR,
        scratch_shapes=[pltpu.VMEM((2, rows * sources, NARROW), F32)],
    )(near, table, traces)


def join_kernel(*refs):
    *in_refs, out_ref = refs
    for k, in_ref in enumerate(in_refs):
        out_ref[:, k] = in_ref[...]


def join(pieces):
    count, *rest = pieces[0].shape
    shape = (count, len(pieces), *rest)
    return call(
        join_kernel,
        jax.ShapeDtypeStruct(shape, BF16),
        0,
        4 * math.prod(shape),
        60,
        in_specs=[VMEM] * len(pieces),
        out_specs=VMEM,
    )(*pieces)


def pick_rows(order_ref, at, count):
    lanes, size = 128, order_ref.shape[1]
    row = order_ref[:, at : at + count].astype(F32)
    column = jnp.broadcast_to(row, (lanes, count)).T
    lane = lax.broadcasted_iota(jnp.int32, (count, lanes), 1).astype(F32)
    picks = [jnp.where(column == lane + float(b), 1.0, 0.0).astype(BF16) for b in range(0, size, lanes)]
    return jnp.concatenate(picks, axis=1)


def rows_of(piece_ref, part):
    owners, _, sources, width = piece_ref.shape
    return piece_ref[:, part].astype(F32).reshape(owners * sources, width).astype(BF16)


def both_of(piece_ref):
    return jnp.concatenate([rows_of(piece_ref, part) for part in range(2)], axis=1)


def off_kernel(order_ref, piece_ref, off_ref):
    half = off_ref.shape[1]
    width = off_ref.shape[2]
    block = dot(pick_rows(order_ref, half, half), both_of(piece_ref)).astype(BF16)
    for part in range(2):
        off_ref[part] = block[:, part * width : (part + 1) * width]


def off_block(order, piece):
    half, width = order.shape[1] // 2, piece.shape[3]
    return call(
        off_kernel,
        jax.ShapeDtypeStruct((2, half, width), BF16),
        8 * half * half * width,
        14 * half * width,
        16,
        in_specs=[VMEM] * 2,
        out_specs=VMEM,
    )(order, piece)


def mix(real, imag):
    row, col = grid_of(real.shape[0])
    diagonal = jnp.sum(jnp.where(row == col, imag, 0.0), axis=0, keepdims=True)
    return jnp.where(row >= col, real, imag).astype(BF16), jnp.broadcast_to(diagonal, (PAD, real.shape[0])).astype(BF16)


def unmix(mixed, diagonal):
    row, col = grid_of(mixed.shape[0])
    turned, mixed, diagonal = turn(mixed), mixed.astype(F32), diagonal.astype(F32)
    real = jnp.where(row >= col, mixed, turned)
    imag = jnp.where(row < col, mixed, jnp.where(row > col, turned, diagonal))
    return real.astype(BF16), imag.astype(BF16)


def wide_kernel(order_ref, piece_ref, square_ref, below_ref, packed_ref):
    both = dot(pick_rows(order_ref, 0, WIDE + NARROW), both_of(piece_ref))
    parts = []
    for part in range(2):
        block = both[:, part * WIDE : (part + 1) * WIDE]
        below_ref[part] = block[WIDE:].astype(BF16)
        parts.append((block[:WIDE] + turn(block[:WIDE].astype(BF16))) * 0.5)
        square_ref[part] = parts[part].astype(BF16)
    packed_ref[:WIDE, :], packed_ref[WIDE:, :] = mix(*parts)


def wide_block(order, piece):
    half = WIDE + NARROW
    return call(
        wide_kernel,
        [jax.ShapeDtypeStruct(shape, BF16) for shape in ((2, WIDE, WIDE), (2, NARROW, WIDE), (WIDE + PAD, WIDE))],
        8 * half * half * WIDE,
        14 * half * WIDE,
        20,
        in_specs=[VMEM] * 2,
        out_specs=[VMEM] * 3,
    )(order, piece)


CUT = 48


def narrow_kernel(order_ref, piece_ref, square_ref, below_ref, own_ref, packed_ref):
    both = dot(pick_rows(order_ref, 0, WIDE + NARROW), both_of(piece_ref))
    corners = []
    for part in range(2):
        block = both[:, part * NARROW : (part + 1) * NARROW]
        beside, corner = block[:WIDE].astype(BF16), block[WIDE:]
        low = ((below_ref[part].astype(F32) + turn(beside)) * 0.5).astype(BF16)
        corners.append((corner + turn(corner.astype(BF16))) * 0.5)
        own_ref[part, :WIDE, :WIDE] = square_ref[part]
        own_ref[part, WIDE:, :WIDE] = low
        own_ref[part, :WIDE, WIDE:] = turn(low).astype(BF16)
        own_ref[part, WIDE:, WIDE:] = corners[part].astype(BF16)
        packed_ref[part * NARROW : (part + 1) * NARROW, :] = low
    mixed, diagonal = mix(*corners)
    at = 2 * NARROW
    packed_ref[at:, :NARROW] = mixed[:CUT]
    packed_ref[at:, NARROW : 2 * NARROW] = mixed[CUT : 2 * CUT]
    packed_ref[at:, 2 * NARROW :] = jnp.concatenate([mixed[2 * CUT :], diagonal], axis=0)


def narrow_block(order, piece, square, below):
    half = WIDE + NARROW
    return call(
        narrow_kernel,
        [jax.ShapeDtypeStruct(shape, BF16) for shape in ((2, half, half), (2 * NARROW + CUT, WIDE))],
        8 * half * half * NARROW,
        14 * half * half,
        20,
        in_specs=[VMEM] * 4,
        out_specs=[VMEM] * 2,
    )(order, piece, square, below)


def unpack(left_wide, left_narrow, wide_ref, narrow_ref):
    squares = unmix(wide_ref[:WIDE, :], wide_ref[WIDE : WIDE + 1, :])
    cuts = narrow_ref[2 * NARROW :, :]
    rest = NARROW - 2 * CUT
    mixed = jnp.concatenate([cuts[:, :NARROW], cuts[:, NARROW : 2 * NARROW], cuts[:rest, 2 * NARROW :]], axis=0)
    corners = unmix(mixed, cuts[rest : rest + 1, 2 * NARROW :])
    for part in range(2):
        low = narrow_ref[part * NARROW : (part + 1) * NARROW, :]
        at = slice(part * WIDE, (part + 1) * WIDE)
        left_wide[:WIDE, at] = squares[part]
        left_wide[WIDE:, at] = low
        at = slice(part * NARROW, (part + 1) * NARROW)
        left_narrow[:WIDE, at] = turn(low).astype(BF16)
        left_narrow[WIDE:, at] = corners[part]


def put_right(right_ref, real, imag):
    rows, cols = real.shape
    right_ref[:rows, :cols] = real
    right_ref[:rows, cols:] = imag
    right_ref[rows:, :cols] = -imag
    right_ref[rows:, cols:] = real


def average(block, turned):
    return ((block.astype(F32) + turn(turned)) * 0.5).astype(BF16)


def early_kernel(own_ref, off_wide, off_narrow, their_wide, right_own, upper_wide, right_wide, part_own, part_other):
    half = own_ref.shape[1]
    put_right(right_own, own_ref[0], own_ref[1])
    lows = []
    for part in range(2):
        off = jnp.concatenate([off_wide[part, :WIDE, :], off_narrow[part, :WIDE, :]], axis=1)
        lows.append(average(off, their_wide[part]))
        upper_wide[:, part * WIDE : (part + 1) * WIDE] = average(their_wide[part], off)
    put_right(right_wide, *lows)
    part_own[...] = dot(right_own[:half, :], right_own[...]) + dot(upper_wide[...], right_wide[...])
    part_other[...] = dot(right_wide[:WIDE, :], right_own[...])


def early(*blocks):
    half = WIDE + NARROW
    shapes = [
        jax.ShapeDtypeStruct((2 * half, 2 * half), BF16),
        jax.ShapeDtypeStruct((half, 2 * WIDE), BF16),
        jax.ShapeDtypeStruct((2 * WIDE, 2 * half), BF16),
        jax.ShapeDtypeStruct((half, 2 * half), F32),
        jax.ShapeDtypeStruct((WIDE, 2 * half), F32),
    ]
    return call(
        early_kernel, shapes, 24 * half**3, 60 * half**2, 24, in_specs=[VMEM] * len(blocks), out_specs=[VMEM] * len(shapes)
    )(*blocks)


def first_kernel(
    scale, off_wide, off_narrow, their_narrow, right_own, right_wide, part_own,
    upper_narrow, right_narrow, square_own, part_other, cube_own, cube_wide, cube_narrow, right_square,
):
    half = off_wide.shape[1]
    lows = []
    for part in range(2):
        off = jnp.concatenate([off_wide[part, WIDE:, :], off_narrow[part, WIDE:, :]], axis=1)
        lows.append(average(off, their_narrow[part]))
        upper_narrow[:, part * NARROW : (part + 1) * NARROW] = average(their_narrow[part], off)
    put_right(right_narrow, *lows)
    square = (scale * (part_own[...] + dot(upper_narrow[...], right_narrow[...]))).astype(BF16)
    square_own[...] = square
    put_right(right_square, square[:, :half], square[:, half:])
    part_other[...] = dot(right_narrow[:NARROW, :], right_own[...])
    cube_own[...] = dot(right_own[:half, :], right_square[...])
    cube_wide[...] = dot(right_wide[:WIDE, :], right_square[...])
    cube_narrow[...] = dot(right_narrow[:NARROW, :], right_square[...])


def first(*blocks):
    half = WIDE + NARROW
    shapes = [
        jax.ShapeDtypeStruct((half, 2 * NARROW), BF16),
        jax.ShapeDtypeStruct((2 * NARROW, 2 * half), BF16),
        jax.ShapeDtypeStruct((half, 2 * half), BF16),
        jax.ShapeDtypeStruct((NARROW, 2 * half), F32),
        jax.ShapeDtypeStruct((half, 2 * half), F32),
        jax.ShapeDtypeStruct((WIDE, 2 * half), F32),
        jax.ShapeDtypeStruct((NARROW, 2 * half), F32),
    ]
    return call(
        functools.partial(first_kernel, 1.0 / math.sqrt(2 * half)),
        shapes,
        22 * half**3,
        60 * half**2,
        28,
        in_specs=[VMEM] * len(blocks),
        out_specs=[VMEM] * len(shapes),
        scratch_shapes=[pltpu.VMEM((2 * half, 2 * half), BF16)],
    )(*blocks)


def second_kernel(
    scale, col_ref, packed_wide, packed_narrow, right_own, square_own, cube_own,
    upper_wide, right_wide, other_wide, cube_wide, upper_narrow, right_narrow, other_narrow, cube_narrow,
    out_ref, left_wide, left_narrow, next_wide, next_narrow, whole_ref, sems,
):
    half = WIDE + NARROW
    unpack(left_wide, left_narrow, packed_wide, packed_narrow)

    def product(wide, narrow):
        return dot(left_wide[...], wide[...]) + dot(left_narrow[...], narrow[...])

    def send(number, values):
        row = pl.multiple_of(lax.rem(col_ref[0] + number, 2) * half, half)
        copies = []
        for part in range(2):
            whole_ref[number, part] = values[:, part * half : (part + 1) * half].astype(BF16)
            copies.append(
                pltpu.make_async_copy(
                    whole_ref.at[number, part], out_ref.at[part, 0, pl.ds(row, half)], sems.at[2 * number + part]
                )
            )
            copies[-1].start()
        return copies

    other = jnp.concatenate([other_wide[...], other_narrow[...]], axis=0)
    square = (scale * (other + product(right_wide, right_narrow))).astype(BF16)
    put_right(next_wide, square[:WIDE, :half], square[:WIDE, half:])
    put_right(next_narrow, square[WIDE:, :half], square[WIDE:, half:])
    cube = scale * (cube_own[...] + dot(upper_wide[...], next_wide[...]) + dot(upper_narrow[...], next_narrow[...]))
    copies = send(0, right_own[:half, :].astype(F32) - square_own[...].astype(F32) + cube)
    other = jnp.concatenate([cube_wide[...], cube_narrow[...]], axis=0)
    cube = scale * (other + product(next_wide, next_narrow))
    low = jnp.concatenate([right_wide[:WIDE, :], right_narrow[:NARROW, :]], axis=0)
    copies += send(1, low.astype(F32) - square.astype(F32) + cube)
    for copy in copies:
        copy.wait()


def second(column_half, *blocks):
    half = WIDE + NARROW
    return call(
        functools.partial(second_kernel, 1.0 / math.sqrt(2 * half)),
        jax.ShapeDtypeStruct((2, 1, 2 * half, half), BF16),
        24 * half**3,
        60 * half**2,
        32,
        in_specs=[SMEM] + [VMEM] * len(blocks),
        out_specs=pl.BlockSpec(memory_space=pl.ANY),
        scratch_shapes=[
            pltpu.VMEM((half, 2 * WIDE), BF16),
            pltpu.VMEM((half, 2 * NARROW), BF16),
            pltpu.VMEM((2 * WIDE, 2 * half), BF16),
            pltpu.VMEM((2 * NARROW, 2 * half), BF16),
            pltpu.VMEM((2, 2, half, half), BF16),
            pltpu.SemaphoreType.DMA((4,)),
        ],
    )(scalar(column_half), *blocks)


def scalar(value):
    return jnp.full((1,), value, jnp.int32)


def swap(piece, groups=None):
    return lax.all_to_all(piece, "freq", split_axis=0, concat_axis=0, tiled=True, axis_index_groups=groups)


def swap_near(value, bits):
    return lax.ppermute(value, "freq", [(i, i ^ bits) for i in range(lax.axis_size("freq"))])


def body(traces, source_row):
    sources, _, samples = traces.shape
    kept = samples // 8
    size = source_row.shape[0]
    assert lax.axis_size("freq") == kept == 128
    column_half = lax.axis_index("col")
    owner = lax.axis_index("freq")
    order = jnp.roll(source_row, -column_half * (size // 2))[None, :]
    source_owner = order // sources
    apart = source_owner ^ owner
    near = (apart // 8 & 1) * 2 + (apart & 1)
    far = source_owner // 16 * 4 + (source_owner // 2 & 3)
    mixed_order = (far * NEAR + near) * sources + order % sources
    wide, *narrow = dft(scalar(owner & NEAR_BITS), dft_table(samples, kept), traces)
    wide = swap(wide.reshape(kept, 2, sources, WIDE))
    for k in range(1, NEAR):
        narrow[k] = swap_near(narrow[k], near_bits(k))
    narrow = join(narrow)
    off_wide = off_block(order, wide)
    their_off_wide = partner(off_wide)
    groups = [[far_owner(i) + near_bits(k) for i in range(kept // NEAR)] for k in range(NEAR)]
    narrow = swap(narrow, groups).reshape(kept, 2, sources, NARROW)
    square, below, packed_wide = wide_block(order, wide)
    packed_wide = partner(packed_wide)
    off_narrow = off_block(mixed_order, narrow)
    their_off_narrow = partner(off_narrow)
    own, packed_narrow = narrow_block(mixed_order, narrow, square, below)
    packed_narrow = partner(packed_narrow)
    right_own, upper_wide, right_wide, part_own, other_wide = early(own, off_wide, off_narrow, their_off_wide)
    upper_narrow, right_narrow, square_own, other_narrow, cube_own, cube_wide, cube_narrow = first(
        off_wide, off_narrow, their_off_narrow, right_own, right_wide, part_own
    )
    return second(
        column_half, packed_wide, packed_narrow, right_own, square_own, cube_own,
        upper_wide, right_wide, other_wide, cube_wide, upper_narrow, right_narrow, other_narrow, cube_narrow,
    )


def solution(mesh):
    in_specs = (P("freq", "col", None), P())
    out_specs = P(None, "freq", None, "col")
    return jax.shard_map(body, mesh=mesh, in_specs=in_specs, out_specs=out_specs, check_vma=False)
```

```python
import functools
import math

import jax
import jax.numpy as jnp
import numpy as np
from jax import lax
from jax.experimental import pallas as pl
from jax.experimental.pallas import tpu as pltpu
from jax.sharding import PartitionSpec as P


BF16 = jnp.bfloat16
F32 = jnp.float32
VMEM = pl.BlockSpec(memory_space=pltpu.VMEM)
SMEM = pl.BlockSpec(memory_space=pltpu.SMEM)
NT = ((1,), (1,))
PAD = 16


def partner(value):
    return lax.ppermute(value, "col", [(0, 1), (1, 0)])


WIDE, NARROW = 384, 128
NEAR, NEAR_BITS = 4, 9


def dft_table(samples, kept):
    phase = np.arange(kept)[:, None] * np.arange(samples)[None, :] % samples
    angle = np.float32(2.0 * math.pi / samples) * phase.astype(np.float32)
    table = np.stack([np.cos(angle), -np.sin(angle)], 1).reshape(2 * kept, samples)
    return jnp.asarray(table / np.sqrt(np.float32(samples)), dtype=BF16)


def dot(a, b, dims=((1,), (0,))):
    return lax.dot_general(a, b, (dims, ((), ())), preferred_element_type=F32)


def grid_of(size):
    return lax.broadcasted_iota(jnp.int32, (size, size), 0), lax.broadcasted_iota(jnp.int32, (size, size), 1)


def turn(block):
    return block.T.astype(F32)


def call(kernel, out_shape, flops, moved, vmem_mib, **rest):
    return pl.pallas_call(
        kernel,
        out_shape=out_shape,
        cost_estimate=pl.CostEstimate(flops=flops, bytes_accessed=moved, transcendentals=0),
        compiler_params=pltpu.CompilerParams(vmem_limit_bytes=vmem_mib << 20),
        **rest,
    )


def far_owner(index):
    return index // 4 * 16 + index % 4 * 2


def near_bits(k):
    return k // 2 * 8 + k % 2


def transform(table_ref, traces_ref, stage_ref):
    sources, width, samples = traces_ref.shape
    rows = table_ref.shape[0]
    value = dot(table_ref[...], traces_ref[...].reshape(sources * width, samples), NT)
    for s in range(sources):
        stage_ref[pl.ds(s, rows, stride=sources), :] = value[:, s * width : (s + 1) * width]


def wide_dft_kernel(table_ref, traces_ref, out_ref, stage_ref):
    transform(table_ref, traces_ref, stage_ref)
    out_ref[...] = stage_ref[...].reshape(out_ref.shape).astype(BF16)


def narrow_dft_kernel(near_ref, table_ref, traces_ref, *rest):
    *narrow_refs, stage_ref = rest
    transform(table_ref, traces_ref, stage_ref)
    _, parts, sources, width = narrow_refs[0].shape
    step = parts * sources
    for k, narrow_ref in enumerate(narrow_refs):
        near = near_ref[0] ^ near_bits(k)
        for index in range(narrow_ref.shape[0]):
            at = pl.multiple_of((far_owner(index) + near) * step, step)
            narrow_ref[index] = stage_ref[pl.ds(at, step), :].reshape(parts, sources, width).astype(BF16)


def wide_dft(table, traces):
    rows, samples = table.shape
    sources, receivers, _ = traces.shape
    assert receivers == WIDE + NARROW
    return call(
        wide_dft_kernel,
        jax.ShapeDtypeStruct((rows, sources, WIDE), BF16),
        2 * rows * samples * sources * WIDE,
        2 * (sources * WIDE * samples + rows * samples + rows * sources * WIDE),
        60,
        grid=(WIDE // NARROW,),
        in_specs=[
            pl.BlockSpec((rows, samples), lambda j: (0, 0)),
            pl.BlockSpec((sources, NARROW, samples), lambda j: (0, j, 0)),
        ],
        out_specs=pl.BlockSpec((rows, sources, NARROW), lambda j: (0, 0, j)),
        scratch_shapes=[pltpu.VMEM((rows * sources, NARROW), F32)],
    )(table, traces)


def narrow_dft(near, table, traces):
    rows, samples = table.shape
    sources = traces.shape[0]
    narrow = (rows // 2 // NEAR, 2, sources, NARROW)
    return call(
        narrow_dft_kernel,
        [jax.ShapeDtypeStruct(narrow, BF16)] * NEAR,
        2 * rows * samples * sources * NARROW,
        2 * (sources * NARROW * samples + rows * samples + rows * sources * NARROW),
        60,
        grid=(1,),
        in_specs=[
            SMEM,
            pl.BlockSpec((rows, samples), lambda j: (0, 0)),
            pl.BlockSpec((sources, NARROW, samples), lambda j: (0, WIDE // NARROW, 0)),
        ],
        out_specs=[pl.BlockSpec(narrow, lambda j: (0, 0, 0, 0))] * NEAR,
        scratch_shapes=[pltpu.VMEM((rows * sources, NARROW), F32)],
    )(near, table, traces)


def join_kernel(*refs):
    *in_refs, out_ref = refs
    for k, in_ref in enumerate(in_refs):
        out_ref[:, k] = in_ref[...]


def join(pieces):
    count, *rest = pieces[0].shape
    shape = (count, len(pieces), *rest)
    return call(
        join_kernel,
        jax.ShapeDtypeStruct(shape, BF16),
        0,
        4 * math.prod(shape),
        60,
        in_specs=[VMEM] * len(pieces),
        out_specs=VMEM,
    )(*pieces)


def pick_rows(order_ref, at, count):
    lanes, size = 128, order_ref.shape[1]
    row = order_ref[:, at : at + count].astype(F32)
    column = jnp.broadcast_to(row, (lanes, count)).T
    lane = lax.broadcasted_iota(jnp.int32, (count, lanes), 1).astype(F32)
    picks = [jnp.where(column == lane + float(b), 1.0, 0.0).astype(BF16) for b in range(0, size, lanes)]
    return jnp.concatenate(picks, axis=1)


def rows_of(piece_ref, part):
    owners, _, sources, width = piece_ref.shape
    return piece_ref[:, part].astype(F32).reshape(owners * sources, width).astype(BF16)


def both_of(piece_ref):
    return jnp.concatenate([rows_of(piece_ref, part) for part in range(2)], axis=1)


def off_kernel(order_ref, piece_ref, off_ref):
    half = off_ref.shape[1]
    width = off_ref.shape[2]
    block = dot(pick_rows(order_ref, half, half), both_of(piece_ref)).astype(BF16)
    for part in range(2):
        off_ref[part] = block[:, part * width : (part + 1) * width]


def off_block(order, piece):
    half, width = order.shape[1] // 2, piece.shape[3]
    return call(
        off_kernel,
        jax.ShapeDtypeStruct((2, half, width), BF16),
        8 * half * half * width,
        14 * half * width,
        16,
        in_specs=[VMEM] * 2,
        out_specs=VMEM,
    )(order, piece)


def mix(real, imag):
    row, col = grid_of(real.shape[0])
    diagonal = jnp.sum(jnp.where(row == col, imag, 0.0), axis=0, keepdims=True)
    return jnp.where(row >= col, real, imag).astype(BF16), jnp.broadcast_to(diagonal, (PAD, real.shape[0])).astype(BF16)


def unmix(mixed, diagonal):
    row, col = grid_of(mixed.shape[0])
    turned, mixed, diagonal = turn(mixed), mixed.astype(F32), diagonal.astype(F32)
    real = jnp.where(row >= col, mixed, turned)
    imag = jnp.where(row < col, mixed, jnp.where(row > col, turned, diagonal))
    return real.astype(BF16), imag.astype(BF16)


def wide_kernel(order_ref, piece_ref, square_ref, below_ref, packed_ref):
    both = dot(pick_rows(order_ref, 0, WIDE + NARROW), both_of(piece_ref))
    parts = []
    for part in range(2):
        block = both[:, part * WIDE : (part + 1) * WIDE]
        below_ref[part] = block[WIDE:].astype(BF16)
        parts.append((block[:WIDE] + turn(block[:WIDE].astype(BF16))) * 0.5)
        square_ref[part] = parts[part].astype(BF16)
    packed_ref[:WIDE, :], packed_ref[WIDE:, :] = mix(*parts)


def wide_block(order, piece):
    half = WIDE + NARROW
    return call(
        wide_kernel,
        [jax.ShapeDtypeStruct(shape, BF16) for shape in ((2, WIDE, WIDE), (2, NARROW, WIDE), (WIDE + PAD, WIDE))],
        8 * half * half * WIDE,
        14 * half * WIDE,
        20,
        in_specs=[VMEM] * 2,
        out_specs=[VMEM] * 3,
    )(order, piece)


CUT = 48


def narrow_kernel(order_ref, piece_ref, square_ref, below_ref, own_ref, packed_ref):
    both = dot(pick_rows(order_ref, 0, WIDE + NARROW), both_of(piece_ref))
    corners = []
    for part in range(2):
        block = both[:, part * NARROW : (part + 1) * NARROW]
        beside, corner = block[:WIDE].astype(BF16), block[WIDE:]
        low = ((below_ref[part].astype(F32) + turn(beside)) * 0.5).astype(BF16)
        corners.append((corner + turn(corner.astype(BF16))) * 0.5)
        own_ref[part, :WIDE, :WIDE] = square_ref[part]
        own_ref[part, WIDE:, :WIDE] = low
        own_ref[part, :WIDE, WIDE:] = turn(low).astype(BF16)
        own_ref[part, WIDE:, WIDE:] = corners[part].astype(BF16)
        packed_ref[part * NARROW : (part + 1) * NARROW, :] = low
    mixed, diagonal = mix(*corners)
    at = 2 * NARROW
    packed_ref[at:, :NARROW] = mixed[:CUT]
    packed_ref[at:, NARROW : 2 * NARROW] = mixed[CUT : 2 * CUT]
    packed_ref[at:, 2 * NARROW :] = jnp.concatenate([mixed[2 * CUT :], diagonal], axis=0)


def narrow_block(order, piece, square, below):
    half = WIDE + NARROW
    return call(
        narrow_kernel,
        [jax.ShapeDtypeStruct(shape, BF16) for shape in ((2, half, half), (2 * NARROW + CUT, WIDE))],
        8 * half * half * NARROW,
        14 * half * half,
        20,
        in_specs=[VMEM] * 4,
        out_specs=[VMEM] * 2,
    )(order, piece, square, below)


def unpack(left_wide, left_narrow, left_square, narrow_ref):
    left_wide[:WIDE, :] = left_square[...]
    cuts = narrow_ref[2 * NARROW :, :]
    rest = NARROW - 2 * CUT
    mixed = jnp.concatenate([cuts[:, :NARROW], cuts[:, NARROW : 2 * NARROW], cuts[:rest, 2 * NARROW :]], axis=0)
    corners = unmix(mixed, cuts[rest : rest + 1, 2 * NARROW :])
    for part in range(2):
        low = narrow_ref[part * NARROW : (part + 1) * NARROW, :]
        at = slice(part * WIDE, (part + 1) * WIDE)
        left_wide[WIDE:, at] = low
        at = slice(part * NARROW, (part + 1) * NARROW)
        left_narrow[:WIDE, at] = turn(low).astype(BF16)
        left_narrow[WIDE:, at] = corners[part]


def put_right(right_ref, real, imag):
    rows, cols = real.shape
    right_ref[:rows, :cols] = real
    right_ref[:rows, cols:] = imag
    right_ref[rows:, :cols] = -imag
    right_ref[rows:, cols:] = real


def average(block, turned):
    return ((block.astype(F32) + turn(turned)) * 0.5).astype(BF16)


def early_kernel(
    own_ref, off_wide, off_narrow, their_wide, packed_wide, right_own, upper_wide, right_wide, left_square, part_own, part_other
):
    half = own_ref.shape[1]
    put_right(right_own, own_ref[0], own_ref[1])
    lows = []
    for part in range(2):
        off = jnp.concatenate([off_wide[part, :WIDE, :], off_narrow[part, :WIDE, :]], axis=1)
        lows.append(average(off, their_wide[part]))
        upper_wide[:, part * WIDE : (part + 1) * WIDE] = average(their_wide[part], off)
    put_right(right_wide, *lows)
    part_own[...] = dot(right_own[:half, :], right_own[...]) + dot(upper_wide[...], right_wide[...])
    squares = unmix(packed_wide[:WIDE, :], packed_wide[WIDE : WIDE + 1, :])
    for part in range(2):
        left_square[:, part * WIDE : (part + 1) * WIDE] = squares[part]
    part_other[...] = dot(right_wide[:WIDE, :], right_own[...]) + dot(left_square[...], right_wide[...])


def early(*blocks):
    half = WIDE + NARROW
    shapes = [
        jax.ShapeDtypeStruct((2 * half, 2 * half), BF16),
        jax.ShapeDtypeStruct((half, 2 * WIDE), BF16),
        jax.ShapeDtypeStruct((2 * WIDE, 2 * half), BF16),
        jax.ShapeDtypeStruct((WIDE, 2 * WIDE), BF16),
        jax.ShapeDtypeStruct((half, 2 * half), F32),
        jax.ShapeDtypeStruct((WIDE, 2 * half), F32),
    ]
    return call(
        early_kernel, shapes, 24 * half**3, 60 * half**2, 24, in_specs=[VMEM] * len(blocks), out_specs=[VMEM] * len(shapes)
    )(*blocks)


def first_kernel(
    scale, off_wide, off_narrow, their_narrow, right_own, right_wide, part_own,
    upper_narrow, right_narrow, square_own, part_other, cube_own, cube_wide, cube_narrow, right_square,
):
    half = off_wide.shape[1]
    lows = []
    for part in range(2):
        off = jnp.concatenate([off_wide[part, WIDE:, :], off_narrow[part, WIDE:, :]], axis=1)
        lows.append(average(off, their_narrow[part]))
        upper_narrow[:, part * NARROW : (part + 1) * NARROW] = average(their_narrow[part], off)
    put_right(right_narrow, *lows)
    square = (scale * (part_own[...] + dot(upper_narrow[...], right_narrow[...]))).astype(BF16)
    square_own[...] = square
    put_right(right_square, square[:, :half], square[:, half:])
    part_other[...] = dot(right_narrow[:NARROW, :], right_own[...])
    cube_own[...] = dot(right_own[:half, :], right_square[...])
    cube_wide[...] = dot(right_wide[:WIDE, :], right_square[...])
    cube_narrow[...] = dot(right_narrow[:NARROW, :], right_square[...])


def first(*blocks):
    half = WIDE + NARROW
    shapes = [
        jax.ShapeDtypeStruct((half, 2 * NARROW), BF16),
        jax.ShapeDtypeStruct((2 * NARROW, 2 * half), BF16),
        jax.ShapeDtypeStruct((half, 2 * half), BF16),
        jax.ShapeDtypeStruct((NARROW, 2 * half), F32),
        jax.ShapeDtypeStruct((half, 2 * half), F32),
        jax.ShapeDtypeStruct((WIDE, 2 * half), F32),
        jax.ShapeDtypeStruct((NARROW, 2 * half), F32),
    ]
    return call(
        functools.partial(first_kernel, 1.0 / math.sqrt(2 * half)),
        shapes,
        22 * half**3,
        60 * half**2,
        28,
        in_specs=[VMEM] * len(blocks),
        out_specs=[VMEM] * len(shapes),
        scratch_shapes=[pltpu.VMEM((2 * half, 2 * half), BF16)],
    )(*blocks)


def second_kernel(
    scale, col_ref, packed_narrow, left_square, right_own, square_own, cube_own,
    upper_wide, right_wide, other_wide, cube_wide, upper_narrow, right_narrow, other_narrow, cube_narrow,
    out_ref, left_wide, left_narrow, next_wide, next_narrow, whole_ref, sems,
):
    half = WIDE + NARROW
    unpack(left_wide, left_narrow, left_square, packed_narrow)

    def product(wide, narrow):
        return dot(left_wide[...], wide[...]) + dot(left_narrow[...], narrow[...])

    def send(number, values):
        row = pl.multiple_of(lax.rem(col_ref[0] + number, 2) * half, half)
        copies = []
        for part in range(2):
            whole_ref[number, part] = values[:, part * half : (part + 1) * half].astype(BF16)
            copies.append(
                pltpu.make_async_copy(
                    whole_ref.at[number, part], out_ref.at[part, 0, pl.ds(row, half)], sems.at[2 * number + part]
                )
            )
            copies[-1].start()
        return copies

    above = other_wide[...] + dot(left_narrow[:WIDE, :], right_narrow[...])
    below = other_narrow[...] + dot(left_wide[WIDE:, :], right_wide[...]) + dot(left_narrow[WIDE:, :], right_narrow[...])
    square = (scale * jnp.concatenate([above, below], axis=0)).astype(BF16)
    put_right(next_wide, square[:WIDE, :half], square[:WIDE, half:])
    put_right(next_narrow, square[WIDE:, :half], square[WIDE:, half:])
    cube = scale * (cube_own[...] + dot(upper_wide[...], next_wide[...]) + dot(upper_narrow[...], next_narrow[...]))
    copies = send(0, right_own[:half, :].astype(F32) - square_own[...].astype(F32) + cube)
    other = jnp.concatenate([cube_wide[...], cube_narrow[...]], axis=0)
    cube = scale * (other + product(next_wide, next_narrow))
    low = jnp.concatenate([right_wide[:WIDE, :], right_narrow[:NARROW, :]], axis=0)
    copies += send(1, low.astype(F32) - square.astype(F32) + cube)
    for copy in copies:
        copy.wait()


def second(column_half, *blocks):
    half = WIDE + NARROW
    return call(
        functools.partial(second_kernel, 1.0 / math.sqrt(2 * half)),
        jax.ShapeDtypeStruct((2, 1, 2 * half, half), BF16),
        24 * half**3,
        60 * half**2,
        32,
        in_specs=[SMEM] + [VMEM] * len(blocks),
        out_specs=pl.BlockSpec(memory_space=pl.ANY),
        scratch_shapes=[
            pltpu.VMEM((half, 2 * WIDE), BF16),
            pltpu.VMEM((half, 2 * NARROW), BF16),
            pltpu.VMEM((2 * WIDE, 2 * half), BF16),
            pltpu.VMEM((2 * NARROW, 2 * half), BF16),
            pltpu.VMEM((2, 2, half, half), BF16),
            pltpu.SemaphoreType.DMA((4,)),
        ],
    )(scalar(column_half), *blocks)


def scalar(value):
    return jnp.full((1,), value, jnp.int32)


def swap(piece, groups=None):
    return lax.all_to_all(piece, "freq", split_axis=0, concat_axis=0, tiled=True, axis_index_groups=groups)


def swap_near(value, bits):
    return lax.ppermute(value, "freq", [(i, i ^ bits) for i in range(lax.axis_size("freq"))])


def body(traces, source_row):
    sources, _, samples = traces.shape
    kept = samples // 8
    size = source_row.shape[0]
    assert lax.axis_size("freq") == kept == 128
    column_half = lax.axis_index("col")
    owner = lax.axis_index("freq")
    order = jnp.roll(source_row, -column_half * (size // 2))[None, :]
    source_owner = order // sources
    apart = source_owner ^ owner
    near = (apart // 8 & 1) * 2 + (apart & 1)
    far = source_owner // 16 * 4 + (source_owner // 2 & 3)
    mixed_order = (far * NEAR + near) * sources + order % sources
    table = dft_table(samples, kept)
    wide = wide_dft(table, traces)
    wide = swap(wide.reshape(kept, 2, sources, WIDE))
    narrow = list(narrow_dft(scalar(owner & NEAR_BITS), table, traces))
    for k in range(1, NEAR):
        narrow[k] = swap_near(narrow[k], near_bits(k))
    narrow = join(narrow)
    off_wide = off_block(order, wide)
    their_off_wide = partner(off_wide)
    groups = [[far_owner(i) + near_bits(k) for i in range(kept // NEAR)] for k in range(NEAR)]
    narrow = swap(narrow, groups).reshape(kept, 2, sources, NARROW)
    square, below, packed_wide = wide_block(order, wide)
    packed_wide = partner(packed_wide)
    off_narrow = off_block(mixed_order, narrow)
    their_off_narrow = partner(off_narrow)
    own, packed_narrow = narrow_block(mixed_order, narrow, square, below)
    packed_narrow = partner(packed_narrow)
    right_own, upper_wide, right_wide, left_square, part_own, other_wide = early(
        own, off_wide, off_narrow, their_off_wide, packed_wide
    )
    upper_narrow, right_narrow, square_own, other_narrow, cube_own, cube_wide, cube_narrow = first(
        off_wide, off_narrow, their_off_narrow, right_own, right_wide, part_own
    )
    return second(
        column_half, packed_narrow, left_square, right_own, square_own, cube_own,
        upper_wide, right_wide, other_wide, cube_wide, upper_narrow, right_narrow, other_narrow, cube_narrow,
    )


def solution(mesh):
    in_specs = (P("freq", "col", None), P())
    out_specs = P(None, "freq", None, "col")
    return jax.shard_map(body, mesh=mesh, in_specs=in_specs, out_specs=out_specs, check_vma=False)
```

```python
import functools
import math

import jax
import jax.numpy as jnp
import numpy as np
from jax import lax
from jax.experimental import pallas as pl
from jax.experimental.pallas import tpu as pltpu
from jax.sharding import PartitionSpec as P


BF16 = jnp.bfloat16
F32 = jnp.float32
VMEM = pl.BlockSpec(memory_space=pltpu.VMEM)
SMEM = pl.BlockSpec(memory_space=pltpu.SMEM)
NT = ((1,), (1,))
PAD = 16


def partner(value):
    return lax.ppermute(value, "col", [(0, 1), (1, 0)])


WIDE, NARROW = 384, 128
NEAR = 16


def dft_table(samples, kept):
    phase = np.arange(kept)[:, None] * np.arange(samples)[None, :] % samples
    angle = np.float32(2.0 * math.pi / samples) * phase.astype(np.float32)
    table = np.stack([np.cos(angle), -np.sin(angle)], 1).reshape(2 * kept, samples)
    return jnp.asarray(table / np.sqrt(np.float32(samples)), dtype=BF16)


def dot(a, b, dims=((1,), (0,))):
    return lax.dot_general(a, b, (dims, ((), ())), preferred_element_type=F32)


def grid_of(size):
    return lax.broadcasted_iota(jnp.int32, (size, size), 0), lax.broadcasted_iota(jnp.int32, (size, size), 1)


def turn(block):
    return block.T.astype(F32)


def call(kernel, out_shape, flops, moved, vmem_mib, **rest):
    return pl.pallas_call(
        kernel,
        out_shape=out_shape,
        cost_estimate=pl.CostEstimate(flops=flops, bytes_accessed=moved, transcendentals=0),
        compiler_params=pltpu.CompilerParams(vmem_limit_bytes=vmem_mib << 20),
        **rest,
    )


def transform(table_ref, traces_ref, stage_ref):
    sources, width, samples = traces_ref.shape
    rows = table_ref.shape[0]
    value = dot(table_ref[...], traces_ref[...].reshape(sources * width, samples), NT)
    for s in range(sources):
        stage_ref[pl.ds(s, rows, stride=sources), :] = value[:, s * width : (s + 1) * width]


def wide_dft_kernel(table_ref, traces_ref, out_ref, stage_ref):
    transform(table_ref, traces_ref, stage_ref)
    out_ref[...] = stage_ref[...].reshape(out_ref.shape).astype(BF16)


def narrow_dft_kernel(near_ref, table_ref, traces_ref, *rest):
    *narrow_refs, stage_ref = rest
    transform(table_ref, traces_ref, stage_ref)
    _, parts, sources, width = narrow_refs[0].shape
    step = parts * sources
    for k, narrow_ref in enumerate(narrow_refs):
        near = near_ref[0] ^ k
        for index in range(narrow_ref.shape[0]):
            at = pl.multiple_of((index * NEAR + near) * step, step)
            narrow_ref[index] = stage_ref[pl.ds(at, step), :].reshape(parts, sources, width).astype(BF16)


def wide_dft(table, traces):
    rows, samples = table.shape
    sources, receivers, _ = traces.shape
    assert receivers == WIDE + NARROW
    return call(
        wide_dft_kernel,
        jax.ShapeDtypeStruct((rows, sources, WIDE), BF16),
        2 * rows * samples * sources * WIDE,
        2 * (sources * WIDE * samples + rows * samples + rows * sources * WIDE),
        60,
        grid=(WIDE // NARROW,),
        in_specs=[
            pl.BlockSpec((rows, samples), lambda j: (0, 0)),
            pl.BlockSpec((sources, NARROW, samples), lambda j: (0, j, 0)),
        ],
        out_specs=pl.BlockSpec((rows, sources, NARROW), lambda j: (0, 0, j)),
        scratch_shapes=[pltpu.VMEM((rows * sources, NARROW), F32)],
    )(table, traces)


def narrow_dft(near, table, traces):
    rows, samples = table.shape
    sources = traces.shape[0]
    narrow = (rows // 2 // NEAR, 2, sources, NARROW)
    return call(
        narrow_dft_kernel,
        [jax.ShapeDtypeStruct(narrow, BF16)] * NEAR,
        2 * rows * samples * sources * NARROW,
        2 * (sources * NARROW * samples + rows * samples + rows * sources * NARROW),
        60,
        grid=(1,),
        in_specs=[
            SMEM,
            pl.BlockSpec((rows, samples), lambda j: (0, 0)),
            pl.BlockSpec((sources, NARROW, samples), lambda j: (0, WIDE // NARROW, 0)),
        ],
        out_specs=[pl.BlockSpec(narrow, lambda j: (0, 0, 0, 0))] * NEAR,
        scratch_shapes=[pltpu.VMEM((rows * sources, NARROW), F32)],
    )(near, table, traces)


def join_kernel(*refs):
    *in_refs, out_ref = refs
    for k, in_ref in enumerate(in_refs):
        out_ref[:, k] = in_ref[...]


def join(pieces):
    count, *rest = pieces[0].shape
    shape = (count, len(pieces), *rest)
    return call(
        join_kernel,
        jax.ShapeDtypeStruct(shape, BF16),
        0,
        4 * math.prod(shape),
        60,
        in_specs=[VMEM] * len(pieces),
        out_specs=VMEM,
    )(*pieces)


def pick_rows(order_ref, at, count):
    lanes, size = 128, order_ref.shape[1]
    row = order_ref[:, at : at + count].astype(F32)
    column = jnp.broadcast_to(row, (lanes, count)).T
    lane = lax.broadcasted_iota(jnp.int32, (count, lanes), 1).astype(F32)
    picks = [jnp.where(column == lane + float(b), 1.0, 0.0).astype(BF16) for b in range(0, size, lanes)]
    return jnp.concatenate(picks, axis=1)


def rows_of(piece_ref, part):
    owners, _, sources, width = piece_ref.shape
    return piece_ref[:, part].astype(F32).reshape(owners * sources, width).astype(BF16)


def both_of(piece_ref):
    return jnp.concatenate([rows_of(piece_ref, part) for part in range(2)], axis=1)


def off_kernel(order_ref, piece_ref, off_ref):
    half = off_ref.shape[1]
    width = off_ref.shape[2]
    block = dot(pick_rows(order_ref, half, half), both_of(piece_ref)).astype(BF16)
    for part in range(2):
        off_ref[part] = block[:, part * width : (part + 1) * width]


def off_block(order, piece):
    half, width = order.shape[1] // 2, piece.shape[3]
    return call(
        off_kernel,
        jax.ShapeDtypeStruct((2, half, width), BF16),
        8 * half * half * width,
        14 * half * width,
        16,
        in_specs=[VMEM] * 2,
        out_specs=VMEM,
    )(order, piece)


def mix(real, imag):
    row, col = grid_of(real.shape[0])
    diagonal = jnp.sum(jnp.where(row == col, imag, 0.0), axis=0, keepdims=True)
    return jnp.where(row >= col, real, imag).astype(BF16), jnp.broadcast_to(diagonal, (PAD, real.shape[0])).astype(BF16)


def unmix(mixed, diagonal):
    row, col = grid_of(mixed.shape[0])
    turned, mixed, diagonal = turn(mixed), mixed.astype(F32), diagonal.astype(F32)
    real = jnp.where(row >= col, mixed, turned)
    imag = jnp.where(row < col, mixed, jnp.where(row > col, turned, diagonal))
    return real.astype(BF16), imag.astype(BF16)


def wide_kernel(order_ref, piece_ref, square_ref, below_ref, packed_ref):
    both = dot(pick_rows(order_ref, 0, WIDE + NARROW), both_of(piece_ref))
    parts = []
    for part in range(2):
        block = both[:, part * WIDE : (part + 1) * WIDE]
        below_ref[part] = block[WIDE:].astype(BF16)
        parts.append((block[:WIDE] + turn(block[:WIDE].astype(BF16))) * 0.5)
        square_ref[part] = parts[part].astype(BF16)
    packed_ref[:WIDE, :], packed_ref[WIDE:, :] = mix(*parts)


def wide_block(order, piece):
    half = WIDE + NARROW
    return call(
        wide_kernel,
        [jax.ShapeDtypeStruct(shape, BF16) for shape in ((2, WIDE, WIDE), (2, NARROW, WIDE), (WIDE + PAD, WIDE))],
        8 * half * half * WIDE,
        14 * half * WIDE,
        20,
        in_specs=[VMEM] * 2,
        out_specs=[VMEM] * 3,
    )(order, piece)


CUT = 48


def narrow_kernel(order_ref, piece_ref, square_ref, below_ref, own_ref, packed_ref):
    both = dot(pick_rows(order_ref, 0, WIDE + NARROW), both_of(piece_ref))
    corners = []
    for part in range(2):
        block = both[:, part * NARROW : (part + 1) * NARROW]
        beside, corner = block[:WIDE].astype(BF16), block[WIDE:]
        low = ((below_ref[part].astype(F32) + turn(beside)) * 0.5).astype(BF16)
        corners.append((corner + turn(corner.astype(BF16))) * 0.5)
        own_ref[part, :WIDE, :WIDE] = square_ref[part]
        own_ref[part, WIDE:, :WIDE] = low
        own_ref[part, :WIDE, WIDE:] = turn(low).astype(BF16)
        own_ref[part, WIDE:, WIDE:] = corners[part].astype(BF16)
        packed_ref[part * NARROW : (part + 1) * NARROW, :] = low
    mixed, diagonal = mix(*corners)
    at = 2 * NARROW
    packed_ref[at:, :NARROW] = mixed[:CUT]
    packed_ref[at:, NARROW : 2 * NARROW] = mixed[CUT : 2 * CUT]
    packed_ref[at:, 2 * NARROW :] = jnp.concatenate([mixed[2 * CUT :], diagonal], axis=0)


def narrow_block(order, piece, square, below):
    half = WIDE + NARROW
    return call(
        narrow_kernel,
        [jax.ShapeDtypeStruct(shape, BF16) for shape in ((2, half, half), (2 * NARROW + CUT, WIDE))],
        8 * half * half * NARROW,
        14 * half * half,
        20,
        in_specs=[VMEM] * 4,
        out_specs=[VMEM] * 2,
    )(order, piece, square, below)


def unpack(left_wide, left_narrow, left_square, narrow_ref):
    left_wide[:WIDE, :] = left_square[...]
    cuts = narrow_ref[2 * NARROW :, :]
    rest = NARROW - 2 * CUT
    mixed = jnp.concatenate([cuts[:, :NARROW], cuts[:, NARROW : 2 * NARROW], cuts[:rest, 2 * NARROW :]], axis=0)
    corners = unmix(mixed, cuts[rest : rest + 1, 2 * NARROW :])
    for part in range(2):
        low = narrow_ref[part * NARROW : (part + 1) * NARROW, :]
        at = slice(part * WIDE, (part + 1) * WIDE)
        left_wide[WIDE:, at] = low
        at = slice(part * NARROW, (part + 1) * NARROW)
        left_narrow[:WIDE, at] = turn(low).astype(BF16)
        left_narrow[WIDE:, at] = corners[part]


def put_right(right_ref, real, imag):
    rows, cols = real.shape
    right_ref[:rows, :cols] = real
    right_ref[:rows, cols:] = imag
    right_ref[rows:, :cols] = -imag
    right_ref[rows:, cols:] = real


def average(block, turned):
    return ((block.astype(F32) + turn(turned)) * 0.5).astype(BF16)


def early_kernel(
    own_ref, off_wide, off_narrow, their_wide, packed_wide, right_own, upper_wide, right_wide, left_square, part_own, part_other
):
    half = own_ref.shape[1]
    put_right(right_own, own_ref[0], own_ref[1])
    lows = []
    for part in range(2):
        off = jnp.concatenate([off_wide[part, :WIDE, :], off_narrow[part, :WIDE, :]], axis=1)
        lows.append(average(off, their_wide[part]))
        upper_wide[:, part * WIDE : (part + 1) * WIDE] = average(their_wide[part], off)
    put_right(right_wide, *lows)
    part_own[...] = dot(right_own[:half, :], right_own[...]) + dot(upper_wide[...], right_wide[...])
    squares = unmix(packed_wide[:WIDE, :], packed_wide[WIDE : WIDE + 1, :])
    for part in range(2):
        left_square[:, part * WIDE : (part + 1) * WIDE] = squares[part]
    part_other[...] = dot(right_wide[:WIDE, :], right_own[...]) + dot(left_square[...], right_wide[...])


def early(*blocks):
    half = WIDE + NARROW
    shapes = [
        jax.ShapeDtypeStruct((2 * half, 2 * half), BF16),
        jax.ShapeDtypeStruct((half, 2 * WIDE), BF16),
        jax.ShapeDtypeStruct((2 * WIDE, 2 * half), BF16),
        jax.ShapeDtypeStruct((WIDE, 2 * WIDE), BF16),
        jax.ShapeDtypeStruct((half, 2 * half), F32),
        jax.ShapeDtypeStruct((WIDE, 2 * half), F32),
    ]
    return call(
        early_kernel, shapes, 24 * half**3, 60 * half**2, 24, in_specs=[VMEM] * len(blocks), out_specs=[VMEM] * len(shapes)
    )(*blocks)


def first_kernel(
    scale, off_wide, off_narrow, their_narrow, right_own, right_wide, part_own,
    upper_narrow, right_narrow, square_own, part_other, cube_own, cube_wide, cube_narrow, right_square,
):
    half = off_wide.shape[1]
    lows = []
    for part in range(2):
        off = jnp.concatenate([off_wide[part, WIDE:, :], off_narrow[part, WIDE:, :]], axis=1)
        lows.append(average(off, their_narrow[part]))
        upper_narrow[:, part * NARROW : (part + 1) * NARROW] = average(their_narrow[part], off)
    put_right(right_narrow, *lows)
    square = (scale * (part_own[...] + dot(upper_narrow[...], right_narrow[...]))).astype(BF16)
    square_own[...] = square
    put_right(right_square, square[:, :half], square[:, half:])
    part_other[...] = dot(right_narrow[:NARROW, :], right_own[...])
    cube_own[...] = dot(right_own[:half, :], right_square[...])
    cube_wide[...] = dot(right_wide[:WIDE, :], right_square[...])
    cube_narrow[...] = dot(right_narrow[:NARROW, :], right_square[...])


def first(*blocks):
    half = WIDE + NARROW
    shapes = [
        jax.ShapeDtypeStruct((half, 2 * NARROW), BF16),
        jax.ShapeDtypeStruct((2 * NARROW, 2 * half), BF16),
        jax.ShapeDtypeStruct((half, 2 * half), BF16),
        jax.ShapeDtypeStruct((NARROW, 2 * half), F32),
        jax.ShapeDtypeStruct((half, 2 * half), F32),
        jax.ShapeDtypeStruct((WIDE, 2 * half), F32),
        jax.ShapeDtypeStruct((NARROW, 2 * half), F32),
    ]
    return call(
        functools.partial(first_kernel, 1.0 / math.sqrt(2 * half)),
        shapes,
        22 * half**3,
        60 * half**2,
        28,
        in_specs=[VMEM] * len(blocks),
        out_specs=[VMEM] * len(shapes),
        scratch_shapes=[pltpu.VMEM((2 * half, 2 * half), BF16)],
    )(*blocks)


def second_kernel(
    scale, col_ref, packed_narrow, left_square, right_own, square_own, cube_own,
    upper_wide, right_wide, other_wide, cube_wide, upper_narrow, right_narrow, other_narrow, cube_narrow,
    out_ref, left_wide, left_narrow, next_wide, next_narrow, whole_ref, sems,
):
    half = WIDE + NARROW
    unpack(left_wide, left_narrow, left_square, packed_narrow)

    def product(wide, narrow):
        return dot(left_wide[...], wide[...]) + dot(left_narrow[...], narrow[...])

    def send(number, values):
        row = pl.multiple_of(lax.rem(col_ref[0] + number, 2) * half, half)
        copies = []
        for part in range(2):
            whole_ref[number, part] = values[:, part * half : (part + 1) * half].astype(BF16)
            copies.append(
                pltpu.make_async_copy(
                    whole_ref.at[number, part], out_ref.at[part, 0, pl.ds(row, half)], sems.at[2 * number + part]
                )
            )
            copies[-1].start()
        return copies

    above = other_wide[...] + dot(left_narrow[:WIDE, :], right_narrow[...])
    below = other_narrow[...] + dot(left_wide[WIDE:, :], right_wide[...]) + dot(left_narrow[WIDE:, :], right_narrow[...])
    square = (scale * jnp.concatenate([above, below], axis=0)).astype(BF16)
    put_right(next_wide, square[:WIDE, :half], square[:WIDE, half:])
    put_right(next_narrow, square[WIDE:, :half], square[WIDE:, half:])
    cube = scale * (cube_own[...] + dot(upper_wide[...], next_wide[...]) + dot(upper_narrow[...], next_narrow[...]))
    copies = send(0, right_own[:half, :].astype(F32) - square_own[...].astype(F32) + cube)
    other = jnp.concatenate([cube_wide[...], cube_narrow[...]], axis=0)
    cube = scale * (other + product(next_wide, next_narrow))
    low = jnp.concatenate([right_wide[:WIDE, :], right_narrow[:NARROW, :]], axis=0)
    copies += send(1, low.astype(F32) - square.astype(F32) + cube)
    for copy in copies:
        copy.wait()


def second(column_half, *blocks):
    half = WIDE + NARROW
    return call(
        functools.partial(second_kernel, 1.0 / math.sqrt(2 * half)),
        jax.ShapeDtypeStruct((2, 1, 2 * half, half), BF16),
        24 * half**3,
        60 * half**2,
        32,
        in_specs=[SMEM] + [VMEM] * len(blocks),
        out_specs=pl.BlockSpec(memory_space=pl.ANY),
        scratch_shapes=[
            pltpu.VMEM((half, 2 * WIDE), BF16),
            pltpu.VMEM((half, 2 * NARROW), BF16),
            pltpu.VMEM((2 * WIDE, 2 * half), BF16),
            pltpu.VMEM((2 * NARROW, 2 * half), BF16),
            pltpu.VMEM((2, 2, half, half), BF16),
            pltpu.SemaphoreType.DMA((4,)),
        ],
    )(scalar(column_half), *blocks)


def scalar(value):
    return jnp.full((1,), value, jnp.int32)


def swap(piece, groups=None):
    return lax.all_to_all(piece, "freq", split_axis=0, concat_axis=0, tiled=True, axis_index_groups=groups)


def swap_near(value, bits):
    return lax.ppermute(value, "freq", [(i, i ^ bits) for i in range(lax.axis_size("freq"))])


def body(traces, source_row):
    sources, _, samples = traces.shape
    kept = samples // 8
    size = source_row.shape[0]
    assert lax.axis_size("freq") == kept == 128
    column_half = lax.axis_index("col")
    owner = lax.axis_index("freq")
    order = jnp.roll(source_row, -column_half * (size // 2))[None, :]
    source_owner = order // sources
    mixed_order = (source_owner ^ owner % NEAR) * sources + order % sources
    table = dft_table(samples, kept)
    wide = wide_dft(table, traces)
    wide = swap(wide.reshape(kept, 2, sources, WIDE))
    narrow = list(narrow_dft(scalar(owner % NEAR), table, traces))
    for k in range(1, NEAR):
        narrow[k] = swap_near(narrow[k], k)
    narrow = join(narrow)
    off_wide = off_block(order, wide)
    their_off_wide = partner(off_wide)
    groups = [[i * NEAR + k for i in range(kept // NEAR)] for k in range(NEAR)]
    narrow = swap(narrow, groups).reshape(kept, 2, sources, NARROW)
    square, below, packed_wide = wide_block(order, wide)
    packed_wide = partner(packed_wide)
    off_narrow = off_block(mixed_order, narrow)
    their_off_narrow = partner(off_narrow)
    own, packed_narrow = narrow_block(mixed_order, narrow, square, below)
    packed_narrow = partner(packed_narrow)
    right_own, upper_wide, right_wide, left_square, part_own, other_wide = early(
        own, off_wide, off_narrow, their_off_wide, packed_wide
    )
    upper_narrow, right_narrow, square_own, other_narrow, cube_own, cube_wide, cube_narrow = first(
        off_wide, off_narrow, their_off_narrow, right_own, right_wide, part_own
    )
    return second(
        column_half, packed_narrow, left_square, right_own, square_own, cube_own,
        upper_wide, right_wide, other_wide, cube_wide, upper_narrow, right_narrow, other_narrow, cube_narrow,
    )


def solution(mesh):
    in_specs = (P("freq", "col", None), P())
    out_specs = P(None, "freq", None, "col")
    return jax.shard_map(body, mesh=mesh, in_specs=in_specs, out_specs=out_specs, check_vma=False)
```
